32 devices in a mesh: groups: 2 (over x), mesh: 16 (over z, y, core).
Axes of the slice: x: 2, y: 2, z: 4, core: 2. Of those that a mesh axis runs over, the one named last changes fastest.
Arguments:
- grid_in: bfloat16 [16384, 474], P(('groups', 'mesh')), parts along dimension 0, may hold values from -6 to 6
- owner: int32 [8192, 1], P('mesh'), may hold values from 0 to 15; in each aligned block of 512 rows (0 to 511, 512 to 1023, ...) at most 64 rows name the same one
- node_slot: int32 [8192], P('mesh'), may hold values from 0 to 255
- mesh_embed: bfloat16 [8192, 512], P(('groups', 'mesh')), parts along dimension 0, may hold values from -6 to 6
- edge_latent: bfloat16 [65536, 512], P(('groups', 'mesh')), parts along dimension 0, may hold values from -6 to 6
- senders: int32 [32768], P('mesh'), may hold values from 0 to 767
- receivers: int32 [32768], P('mesh'), may hold values from 0 to 255
- send_list: int32 [256, 32], P('mesh'), may hold values from 0 to 255
- w_grid_first: bfloat16 [474, 512], replicated, may hold values from -0.25 to 0.25
- w_grid_second: bfloat16 [512, 512], replicated, may hold values from -0.25 to 0.25
- w_enc_first: bfloat16 [1024, 512], replicated, may hold values from -0.1875 to 0.1875
- w_enc_second: bfloat16 [512, 512], replicated, may hold values from -0.25 to 0.25
- w_send: bfloat16 [512, 512], replicated, may hold values from -0.15625 to 0.15625
- w_recv: bfloat16 [512, 512], replicated, may hold values from -0.15625 to 0.15625
- w_edge: bfloat16 [512, 512], replicated, may hold values from -0.15625 to 0.15625
- w_message: bfloat16 [512, 512], replicated, may hold values from -0.25 to 0.25
- w_proc_first: bfloat16 [1024, 512], replicated, may hold values from -0.1875 to 0.1875
- w_proc_second: bfloat16 [512, 512], replicated, may hold values from -0.25 to 0.25
Outputs:
- mesh_out: bfloat16 [8192, 512], P(('groups', 'mesh')), parts along dimension 0
The draws below stay inside these ranges and needn't reach their ends.
There are 2 independent parts, one for each index of `groups`. The reference program is written for one: setup_inputs(seed, part) draws one part's arguments, and reference() takes and returns one part's arrays. A program takes and returns all parts, laid end to end along the dimension named above; an argument that names none is the same for every part. Nothing has to cross between parts.
Inputs may be any that keep to these rules, and one draw needn't show every extreme that they name: Among the grid points of one device at most 64 have the same owner, and some device has exactly 64 with one owner. Grid point g feeds node row node_slot[g] of device owner[g]. `senders`: A sender below 256 is a node row of the edge's own device; a sender 256 + p * 32 + j is row send_list[p * 16 + q, j] of device p, where q is the edge's device. `receivers`: edge k lies on device k // 2048; its receiver is a node row of that device. `send_list`: row p * 16 + q lists the 32 node rows of device p sent to device q.
All inputs are finite; a program needn't handle non-finite values.
Results may differ from the reference program's by a relative error of at most 0.0095.
Values may be sent and summed in bfloat16 or wider, within the bound.
A program may use at most 64 MiB of HBM per device.

```python
import math
import jax
import jax.numpy as jnp
import numpy as np
from jax import lax

D = 512
C_IN = 474
G_DEV = 512
NODE_DEV = 256
HALO_DEV = 512
CAP = 64
HCAP = 32
EDGE_DEV = 2048
GRID = 8192
NODES = 4096
EDGES = 32768
PAIRS = 256
N_MESH = 16


def plant(result, own_key, low, top_value):
    extent = result.shape
    place = [jax.random.randint(jax.random.fold_in(own_key, axis), (), 0, extent[axis]) for axis in range(len(extent))]
    result = result.at[tuple(place)].set(low)
    longest = extent.index(max(extent))
    place[longest] = (place[longest] + 1) % extent[longest]
    return result.at[tuple(place)].set(top_value)


def shard_levels(key, dims, pieces, smallest, largest):
    gain = 1.0
    for axis_at, blocks in pieces:
        steps = jax.random.uniform(jax.random.fold_in(jax.random.fold_in(key, 6), axis_at), (blocks,), jnp.float32, smallest / len(pieces), largest / len(pieces))
        gain = gain * jnp.repeat(jnp.exp(steps), dims[axis_at] // blocks).reshape((-1,) + (1,) * (len(dims) - 1 - axis_at))
    return gain


def deal_out(rng, own, number, rows, count, top, most, slope):
    order = jax.random.permutation(rng, count)
    crowded, usual = portions_of(count, rows * top, most, slope, True), portions_of(count, rows * top, most, slope, False)
    places = jnp.arange(count)

    def named(tallies, turn):
        used = int((tallies > 0).sum())
        fixed = max(1, used // 4)
        passed = fixed + (places - fixed + turn * (used - fixed)) % max(1, count - fixed)
        return jnp.zeros((count,), jnp.int32).at[order[jnp.where(places < fixed, places, passed)]].set(jnp.asarray(tallies, jnp.int32))

    tallies = jnp.where(number % 4 == 0, named(crowded, number // 4), named(usual, number - number // 4 - 1))
    mixed = jax.random.permutation(jax.random.fold_in(own, 3), count)
    source_of, receiver = mixed[0:count // 2 * 2:2], mixed[1:count // 2 * 2:2]
    room = jnp.minimum(tallies[source_of] - 1, most - tallies[receiver]) // 2
    room = jnp.where((source_of == order[0]) | (receiver == order[0]) | (tallies[receiver] == 0), 0, jnp.maximum(room, 0))
    passed = jax.random.randint(jax.random.fold_in(own, 4), (count // 2,), 0, 1 << 20) % (room + 1)
    tallies = tallies.at[source_of].add(-passed).at[receiver].add(passed)
    items = jnp.searchsorted(jnp.cumsum(tallies), jnp.arange(rows * top), side="right").astype(jnp.int32)
    grid = items.reshape(top, rows).T
    grid = grid[jax.random.permutation(jax.random.fold_in(own, 1), rows)]
    turn = jax.random.randint(jax.random.fold_in(own, 2), (rows, 1), 0, top)
    return jnp.take_along_axis(grid, (jnp.arange(top)[None, :] + turn) % top, axis=1)


def portions_of(count, total, limit, lean, full):
    weights = [(1 << 20) // math.isqrt(standing ** lean) + 1 for standing in range(1, count + 1)]
    largest = limit if full else min(limit, max(-(-total // count), total * weights[0] // sum(weights)))
    least = 1 if total - largest >= count - 1 else 0
    counts, surplus = [largest] + [least] * (count - 1), total - largest - least * (count - 1)
    while surplus > 0:
        movable = [i for i in range(1, count) if counts[i] < largest] or [i for i in range(1, count) if counts[i] < limit]
        whole, left = sum([weights[i] for i in movable]), surplus
        for i in movable:
            extra = min(limit - counts[i], max(1, left * weights[i] // whole), surplus)
            counts[i] = counts[i] + extra
            surplus = surplus - extra
    return np.array(counts)


def noise(key, shape, scale, limit, cuts=(), held_as=jnp.bfloat16):
    values = jax.random.normal(key, shape, jnp.float32) * scale
    if len(cuts) > 0:
        values = shard_levels(key, shape, cuts, -0.22, 0.18) * values
    return jnp.clip(values, min=-limit, max=limit).astype(held_as)


def setup_inputs(seed: int = 0, part: int = 0) -> dict:
    streams_of = jax.random.split(jax.random.key(seed), 19)
    own_keys = jax.random.split(jax.random.fold_in(streams_of[18], part), 19)
    grid_in = noise(own_keys[0], (GRID, C_IN), 1.0, 6.0, ((0, 16),))
    owner_keys = jax.random.split(jax.random.fold_in(streams_of[1], 1), GRID // G_DEV)
    owner_turns = jax.random.permutation(jax.random.fold_in(streams_of[1], 3), GRID // G_DEV)
    owner = jax.vmap(lambda own, number: deal_out(jax.random.fold_in(streams_of[1], 2), own, number, G_DEV, N_MESH, 1, CAP, 2))(owner_keys, owner_turns).reshape((GRID, 1))
    node_slot = plant(jax.random.randint(streams_of[2], (GRID,), 0, NODE_DEV), jax.random.fold_in(streams_of[2], 1), 0, NODE_DEV - 1).astype(jnp.int32)
    mesh_embed = noise(own_keys[3], (NODES, D), 1.0, 6.0, ((0, 16),))
    edge_latent = noise(own_keys[4], (EDGES, D), 1.0, 6.0, ((0, 16),))
    senders = plant(jax.random.randint(streams_of[5], (EDGES,), 0, NODE_DEV + HALO_DEV), jax.random.fold_in(streams_of[5], 1), 0, (NODE_DEV + HALO_DEV) - 1).astype(jnp.int32)
    receivers = plant(jax.random.randint(streams_of[6], (EDGES,), 0, NODE_DEV), jax.random.fold_in(streams_of[6], 1), 0, NODE_DEV - 1).astype(jnp.int32)
    send_list = plant(jax.random.randint(streams_of[7], (PAIRS, HCAP), 0, NODE_DEV), jax.random.fold_in(streams_of[7], 1), 0, NODE_DEV - 1).astype(jnp.int32)
    w_grid_first = noise(streams_of[8], (C_IN, D), C_IN ** -0.5, 0.25)
    w_grid_second = noise(streams_of[9], (D, D), D ** -0.5, 0.25)
    w_enc_first = noise(streams_of[10], (2 * D, D), (2 * D) ** -0.5, 0.1875)
    w_enc_second = noise(streams_of[11], (D, D), D ** -0.5, 0.25)
    w_send = noise(streams_of[12], (D, D), (3 * D) ** -0.5, 0.15625)
    w_recv = noise(streams_of[13], (D, D), (3 * D) ** -0.5, 0.15625)
    w_edge = noise(streams_of[14], (D, D), (3 * D) ** -0.5, 0.15625)
    w_message = noise(streams_of[15], (D, D), D ** -0.5, 0.25)
    w_proc_first = noise(streams_of[16], (2 * D, D), (2 * D) ** -0.5, 0.1875)
    w_proc_second = noise(streams_of[17], (D, D), D ** -0.5, 0.25)
    return dict(grid_in=grid_in, owner=owner, node_slot=node_slot, mesh_embed=mesh_embed, edge_latent=edge_latent, senders=senders, receivers=receivers, send_list=send_list, w_grid_first=w_grid_first, w_grid_second=w_grid_second, w_enc_first=w_enc_first, w_enc_second=w_enc_second, w_send=w_send, w_recv=w_recv, w_edge=w_edge, w_message=w_message, w_proc_first=w_proc_first, w_proc_second=w_proc_second)


def layer_norm(values):
    center = values - lax.optimization_barrier(jnp.mean(values, -1, keepdims=True))
    spread = lax.optimization_barrier(jnp.mean(center * center, -1, keepdims=True))
    return center * lax.rsqrt(spread + 1e-05)

def embed_grid(grid_rows, w_first, w_second):
    hidden = jax.nn.silu(jnp.dot(grid_rows, w_first, preferred_element_type=jnp.float32)).astype(jnp.bfloat16)
    return layer_norm(jnp.dot(hidden, w_second, preferred_element_type=jnp.float32)).astype(jnp.bfloat16)

def update_nodes(state, gathered, w_first, w_second):
    joined = jnp.concatenate([state.astype(jnp.float32), gathered], -1)
    normed = layer_norm(joined).astype(jnp.bfloat16)
    hidden = jax.nn.silu(jnp.dot(normed, w_first, preferred_element_type=jnp.float32)).astype(jnp.bfloat16)
    return (state.astype(jnp.float32) + jnp.dot(hidden, w_second, preferred_element_type=jnp.float32)).astype(jnp.bfloat16)

def reference(grid_in, owner, node_slot, mesh_embed, edge_latent, senders, receivers, send_list, w_grid_first, w_grid_second, w_enc_first, w_enc_second, w_send, w_recv, w_edge, w_message, w_proc_first, w_proc_second):
    grid_blocks = grid_in.reshape(N_MESH, G_DEV, C_IN)
    destination = (owner[:, 0] * NODE_DEV + node_slot).astype(jnp.int32).reshape(N_MESH, G_DEV)

    def add_grid(running, block):
        block_rows, block_dest = block
        latent = embed_grid(block_rows, w_grid_first, w_grid_second)
        return (running + jax.ops.segment_sum(latent.astype(jnp.float32), block_dest, num_segments=NODES), None)
    g2m_sum, _ = lax.scan(add_grid, jnp.zeros((NODES, D), jnp.float32), (grid_blocks, destination))
    mesh_latent = update_nodes(mesh_embed, g2m_sum, w_enc_first, w_enc_second)
    device_of = (jnp.arange(EDGES, dtype=jnp.int32) // EDGE_DEV).astype(jnp.int32)
    global_recv = (device_of * NODE_DEV + receivers).astype(jnp.int32)
    halo_pos = jnp.maximum(senders - NODE_DEV, 0).astype(jnp.int32)
    source_peer = (halo_pos // HCAP).astype(jnp.int32)
    source_slot = (halo_pos % HCAP).astype(jnp.int32)
    remote = source_peer * NODE_DEV + send_list[source_peer * N_MESH + device_of, source_slot]
    global_send = jnp.where(senders < NODE_DEV, device_of * NODE_DEV + senders, remote).astype(jnp.int32)
    edge_blocks = edge_latent.reshape(N_MESH, EDGE_DEV, D)
    send_blocks = global_send.reshape(N_MESH, EDGE_DEV)
    recv_blocks = global_recv.reshape(N_MESH, EDGE_DEV)

    def add_edges(running, block):
        block_edges, block_send, block_recv = block
        pre = jnp.dot(mesh_latent[block_send], w_send, preferred_element_type=jnp.float32)
        pre = pre + jnp.dot(mesh_latent[block_recv], w_recv, preferred_element_type=jnp.float32)
        pre = pre + jnp.dot(block_edges, w_edge, preferred_element_type=jnp.float32)
        hidden = jax.nn.silu(pre).astype(jnp.bfloat16)
        message = jnp.dot(hidden, w_message, preferred_element_type=jnp.float32)
        return (running + jax.ops.segment_sum(message, block_recv, num_segments=NODES), None)
    node_sum, _ = lax.scan(add_edges, jnp.zeros((NODES, D), jnp.float32), (edge_blocks, send_blocks, recv_blocks))
    return update_nodes(mesh_latent, node_sum, w_proc_first, w_proc_second)
```

```python
import functools

import jax
import jax.numpy as jnp
from jax import lax
from jax.experimental import pallas as pl
from jax.experimental.pallas import tpu as pltpu
from jax.sharding import PartitionSpec as P

F32 = jnp.float32
BF16 = jnp.bfloat16
MESH = pl.DeviceIdType.MESH
GROUP = 256
CHUNK = 256
LANES = 128
DIRECT = 1
HALO_ORDER = (1, 0, 2, 3)


def dot(left, right):
    return jnp.dot(left, right, preferred_element_type=F32)


def silu(x):
    half = 0.5 * x
    return half * jnp.tanh(half) + half


def normalize(values):
    center = values - jnp.mean(values, -1, keepdims=True)
    spread = jnp.mean(center * center, -1, keepdims=True)
    return center * lax.rsqrt(spread + 1e-05)


def hot(flags):
    return jnp.where(flags, 1.0, 0.0).astype(BF16)


def update(state, gathered, w_first, w_second):
    width = state.shape[1]
    rows = state.astype(F32)
    mean = (
        jnp.sum(rows, -1, keepdims=True) + jnp.sum(gathered, -1, keepdims=True)
    ) / (2 * width)
    low, high = rows - mean, gathered - mean
    spread = (
        jnp.sum(low * low, -1, keepdims=True) + jnp.sum(high * high, -1, keepdims=True)
    ) / (2 * width)
    scale = lax.rsqrt(spread + 1e-05)
    hidden = dot((low * scale).astype(BF16), w_first[:width, :])
    hidden = hidden + dot((high * scale).astype(BF16), w_first[width:, :])
    return (rows + dot(silu(hidden).astype(BF16), w_second[...])).astype(BF16)


def kernel(n, cap, hcap, *refs):
    hbm = refs[:18]
    out_ref = refs[18]
    (
        grid_in,
        owner,
        node_slot,
        embed,
        edges,
        senders,
        receivers,
        send_list,
        w_grid_first,
        w_grid_second,
        w_enc_first,
        w_enc_second,
        w_send,
        w_recv,
        w_edge,
        w_message,
        w_proc_first,
        w_proc_second,
    ) = vmem = refs[19:37]
    (
        latent,
        outgoing,
        arrived,
        ids_out,
        ids_in,
        pre,
        local_table,
        near_hot,
        halo_hot,
        node_hot,
        list_hot,
        halo_out,
        halo_in,
        relay_out,
        relay_in,
        relay_send,
        relay_recv,
        load_sem,
        row_send,
        row_recv,
        id_send,
        id_recv,
        halo_send,
        halo_recv,
    ) = refs[37:]
    grid_count = grid_in.shape[1]
    nodes, width = embed.shape
    edge_count = edges.shape[0]
    me = lax.axis_index("mesh")

    half, quarter, chips = n // 2, n // 4, n // 8
    q, place_in = me // quarter, me % quarter
    h = q // 2
    mine = me % half
    core = place_in % 2
    inner = (q + 1) // 2 % 2
    far_inner, far_outer, near_other = 2 - h, 3 - 3 * h, 4 * h + 1 - q
    near_inner = 1 + h
    other = lax.rem(me + half, n)
    by_class = (far_inner, far_outer, near_other, q)

    def column(j):
        return lax.rem(place_in // 2 + j % chips, chips) * 2 + j // chips

    loads = [
        pltpu.make_async_copy(source, target, load_sem.at[i])
        for i, (source, target) in enumerate(zip(hbm, vmem))
    ]
    for i in (0, 8, 1, 2, 9, 14, 4, 3, 10, 11, 7, 12, 13, 5, 6, 15, 16, 17):
        loads[i].start()
    barrier = pltpu.get_barrier_semaphore()
    for t in range(1, n):
        pl.semaphore_signal(
            barrier, inc=1, device_id={"mesh": lax.rem(me + t, n)}, device_id_type=MESH
        )

    loads[1].wait()
    loads[2].wait()
    block = lax.broadcasted_iota(jnp.int32, (n, 1), 0)
    kind, j = block // quarter, block % quarter
    target = jnp.where(
        kind < 2,
        jnp.where(kind == 0, far_inner, far_outer),
        jnp.where(kind == 2, near_other, q),
    )
    target = target * quarter + column(j)
    flags = jnp.where(target == owner[...], 1.0, 0.0)
    earlier = hot(
        lax.broadcasted_iota(jnp.int32, (grid_count, grid_count), 0)
        < lax.broadcasted_iota(jnp.int32, (grid_count, grid_count), 1)
    )
    rank = dot(flags.astype(BF16), earlier) + (block * cap).astype(F32)
    place = jnp.sum(flags * rank, 0, keepdims=True).astype(jnp.int32)
    slots = (flags * (node_slot[...] + 1).astype(F32)).astype(BF16)
    per_group = GROUP // cap
    lane_hot = hot(
        lax.broadcasted_iota(jnp.int32, (GROUP, grid_count), 0)
        == place % cap + mine % per_group * cap
    )
    ids = lax.dot_general(slots, lane_hot, (((1,), (1,)), ((), ())), preferred_element_type=F32)
    for t in range(n):
        ids_out[t] = ids[t : t + 1, :]

    loads[0].wait()
    loads[8].wait()
    loads[9].wait()
    hidden = lax.dot_general(
        grid_in[...], w_grid_first[...], (((0,), (0,)), ((), ())), preferred_element_type=F32
    )
    hidden = silu(hidden).astype(BF16)
    latent[...] = normalize(dot(hidden, w_grid_second[...])).astype(BF16)

    pl.semaphore_wait(barrier, n - 1)

    def row_copies(b, kind, slot, receiver):
        return (
            pltpu.make_async_remote_copy(
                src_ref=ids_out.at[b],
                dst_ref=ids_in.at[kind, slot],
                send_sem=id_send.at[b],
                recv_sem=id_recv.at[kind, slot],
                device_id={"mesh": receiver},
                device_id_type=MESH,
            ),
            pltpu.make_async_remote_copy(
                src_ref=outgoing.at[b],
                dst_ref=arrived.at[kind, slot],
                send_sem=row_send.at[b],
                recv_sem=row_recv.at[kind, slot],
                device_id={"mesh": receiver},
                device_id_type=MESH,
            ),
        )

    sent_rows = []
    for b in range(n):
        if b % per_group == 0:
            pack = hot(
                lax.broadcasted_iota(jnp.int32, (GROUP, grid_count), 0) + b * cap == place
            )
            packed = dot(pack, latent[...]).astype(BF16)
            outgoing[b : b + per_group] = packed.reshape(per_group, cap, width)
        kind, j = b // quarter, b % quarter
        col = column(j)
        if kind == 0:
            receiver = near_inner * quarter + col
        elif kind == 1:
            receiver = jnp.where(
                jnp.int32(j // chips) < DIRECT, far_outer * quarter, near_inner * quarter
            ) + col
        else:
            receiver = by_class[kind] * quarter + col
        slot_kind = min(kind, 2)
        copies = row_copies(b, slot_kind, mine, receiver)
        if j % chips == 0 and (kind != 2) and not (kind == 1 and j // chips < DIRECT):
            own = (core == j // chips) & (True if kind == 3 else inner == 1)
            sent_rows.append((copies, own))

            @pl.when(own)
            def _():
                ids_in[slot_kind, mine] = ids_out[b]
                arrived[slot_kind, mine] = outgoing[b]

            @pl.when(jnp.logical_not(own))
            def _():
                copies[0].start()
                copies[1].start()
        else:
            sent_rows.append((copies, None))
            copies[0].start()
            copies[1].start()

    loads[14].wait()
    loads[4].wait()
    for chunk in range(edge_count // CHUNK):
        rows = pl.ds(chunk * CHUNK, CHUNK)
        pre[rows, :] = dot(edges[rows, :], w_edge[...])

    loads[5].wait()
    loads[6].wait()
    loads[7].wait()
    sender_columns = jnp.transpose(senders[...])
    receiver_columns = jnp.transpose(receivers[...])
    list_columns = jnp.transpose(send_list[...])
    near_iota = lax.broadcasted_iota(jnp.int32, (LANES, nodes), 1)
    lane = lax.broadcasted_iota(jnp.int32, (1, n * hcap), 1)
    halo_place = nodes + lax.rem(lane + h * (half * hcap), n * hcap)
    node_iota = lax.broadcasted_iota(jnp.int32, (nodes, LANES), 0)
    for part in range(edge_count // LANES):
        rows = pl.ds(part * LANES, LANES)
        sender = sender_columns[:, part : part + 1]
        receiver = receiver_columns[:, part : part + 1]
        near_hot[rows, :nodes] = hot(sender == near_iota)
        near_hot[rows, nodes:] = hot(receiver == near_iota)
        halo_hot[rows, :] = hot(sender == halo_place)
        node_hot[:, part * LANES : (part + 1) * LANES] = hot(
            receivers[part : part + 1, :] == node_iota
        )
    list_iota = lax.broadcasted_iota(jnp.int32, (hcap, nodes), 1)
    for p in range(n):
        list_hot[p * hcap : (p + 1) * hcap, :] = hot(list_columns[:, p : p + 1] == list_iota)

    slot_iota = lax.broadcasted_iota(jnp.int32, (nodes, GROUP), 0).astype(F32) + 1.0

    def await_rows(kind, slot):
        copies = row_copies(0, kind, slot, other)
        copies[0].wait_recv()
        copies[1].wait_recv()

    def collect(kind, all_remote):
        total = jnp.zeros((nodes, width), F32)
        for first in range(0, half, per_group):
            named = jnp.zeros((1, GROUP), F32)
            for s in range(first, first + per_group):

                @pl.when(all_remote | (mine != s))
                def _():
                    await_rows(kind, s)

                named = named + ids_in[kind, s]
            total = total + dot(
                hot(slot_iota == named),
                arrived[kind, first : first + per_group].reshape(GROUP, width),
            )
        return total

    def relay(i, receiver):
        return pltpu.make_async_remote_copy(
            src_ref=relay_out.at[i],
            dst_ref=relay_in,
            send_sem=relay_send.at[i],
            recv_sem=relay_recv.at[0],
            device_id={"mesh": receiver},
            device_id_type=MESH,
        )

    relays = (relay(0, far_inner * quarter + place_in), relay(1, far_outer * quarter + place_in))
    direct = jnp.where(core < DIRECT, 1, 0)

    @pl.when(inner == 1)
    def _():
        relay_out[0] = collect(0, False).astype(BF16)
        relays[0].start()

    @pl.when(inner * (1 - direct) == 1)
    def _():
        relay_out[1] = collect(1, False).astype(BF16)
        relays[1].start()

    @pl.when((1 - inner) * direct == 1)
    def _():
        relay_in[...] = collect(1, True).astype(BF16)

    gathered = collect(2, False)

    @pl.when((1 - inner) * direct == 0)
    def _():
        relays[0].wait_recv()

    gathered = gathered + relay_in[...].astype(F32)

    for i in (3, 10, 11, 12, 13):
        loads[i].wait()
    state = update(embed[...], gathered, w_enc_first, w_enc_second)
    sent = dot(state, w_send[...]).astype(BF16)
    halo_out[...] = dot(list_hot[...], sent).astype(BF16).reshape(n, hcap, width)

    def halo_copy(b, slot, receiver):
        return pltpu.make_async_remote_copy(
            src_ref=halo_out.at[receiver],
            dst_ref=halo_in.at[slot],
            send_sem=halo_send.at[b],
            recv_sem=halo_recv.at[slot],
            device_id={"mesh": receiver},
            device_id_type=MESH,
        )

    sent_halos = []
    for b in range(n):
        kind, j = HALO_ORDER[b // quarter], b % quarter
        receiver = by_class[kind] * quarter + column(j)
        copy = halo_copy(b, mine + half if kind < 2 else mine, receiver)
        if kind == 3 and j % chips == 0:
            own = core == j // chips
            sent_halos.append((copy, own))

            @pl.when(jnp.logical_not(own))
            def _():
                copy.start()
        else:
            sent_halos.append((copy, None))
            copy.start()
    halo_in[mine] = halo_out[me]
    local_table[:nodes, :] = sent
    local_table[nodes:, :] = dot(state, w_recv[...]).astype(BF16)
    for chunk in range(edge_count // CHUNK):
        rows = pl.ds(chunk * CHUNK, CHUNK)
        pre[rows, :] += dot(near_hot[rows, :], local_table[...])

    inner_rows = half * hcap
    for s in range(half):

        @pl.when(mine != s)
        def _():
            halo_copy(0, s, other).wait_recv()

    halo = halo_in[:half].reshape(inner_rows, width)
    for chunk in range(edge_count // CHUNK):
        rows = pl.ds(chunk * CHUNK, CHUNK)
        pre[rows, :] += dot(halo_hot[rows, :inner_rows], halo)
    for s in range(half, n):
        halo_copy(0, s, other).wait_recv()
    halo = halo_in[half:].reshape(inner_rows, width)
    summed = jnp.zeros((nodes, width), F32)
    for chunk in range(edge_count // CHUNK):
        rows = pl.ds(chunk * CHUNK, CHUNK)
        edge_pre = pre[rows, :] + dot(halo_hot[rows, inner_rows:], halo)
        summed = summed + dot(
            node_hot[:, chunk * CHUNK : (chunk + 1) * CHUNK], silu(edge_pre).astype(BF16)
        )
    for i in (15, 16, 17):
        loads[i].wait()
    node_sum = dot(summed.astype(BF16), w_message[...])
    out_ref[...] = update(state, node_sum, w_proc_first, w_proc_second)

    @pl.when(inner == 1)
    def _():
        relays[0].wait_send()

    @pl.when(inner * (1 - direct) == 1)
    def _():
        relays[1].wait_send()

    for copies, own in sent_rows:
        if own is None:
            copies[0].wait_send()
            copies[1].wait_send()
        else:

            @pl.when(jnp.logical_not(own))
            def _():
                copies[0].wait_send()
                copies[1].wait_send()

    for copy, own in sent_halos:
        if own is None:
            copy.wait_send()
        else:

            @pl.when(jnp.logical_not(own))
            def _():
                copy.wait_send()


def per_device(
    grid_in, owner, node_slot, mesh_embed, edge_latent, senders, receivers, send_list, *weights
):
    n = lax.axis_size("mesh")
    grid_count = grid_in.shape[0]
    nodes, width = mesh_embed.shape
    edge_count = edge_latent.shape[0]
    list_size = send_list.shape[1]
    cap = max(16, 2 * grid_count // n)
    hcap = max(16, list_size)
    if hcap != list_size:
        beyond = jnp.maximum(senders - nodes, 0)
        moved = nodes + beyond // list_size * hcap + beyond % list_size
        senders = jnp.where(senders < nodes, senders, moved)
        send_list = jnp.pad(send_list, ((0, 0), (0, hcap - list_size)))
    inputs = (
        grid_in.T,
        owner.reshape(1, grid_count),
        node_slot.reshape(1, grid_count),
        mesh_embed,
        edge_latent,
        senders.reshape(edge_count // LANES, LANES),
        receivers.reshape(edge_count // LANES, LANES),
        send_list,
    ) + weights
    dma = pltpu.SemaphoreType.DMA
    scratch = [pltpu.VMEM(x.shape, x.dtype) for x in inputs] + [
        pltpu.VMEM((grid_count, width), BF16),
        pltpu.VMEM((n, cap, width), BF16),
        pltpu.VMEM((3, n // 2, cap, width), BF16),
        pltpu.VMEM((n, 1, GROUP), F32),
        pltpu.VMEM((3, n // 2, 1, GROUP), F32),
        pltpu.VMEM((edge_count, width), F32),
        pltpu.VMEM((2 * nodes, width), BF16),
        pltpu.VMEM((edge_count, 2 * nodes), BF16),
        pltpu.VMEM((edge_count, n * hcap), BF16),
        pltpu.VMEM((nodes, edge_count), BF16),
        pltpu.VMEM((n * hcap, nodes), BF16),
        pltpu.VMEM((n, hcap, width), BF16),
        pltpu.VMEM((n, hcap, width), BF16),
        pltpu.VMEM((2, nodes, width), BF16),
        pltpu.VMEM((nodes, width), BF16),
        dma((2,)),
        dma((1,)),
        dma((len(inputs),)),
        dma((n,)),
        dma((3, n // 2)),
        dma((n,)),
        dma((3, n // 2)),
        dma((n,)),
        dma((n,)),
    ]
    return pl.pallas_call(
        functools.partial(kernel, n, cap, hcap),
        out_shape=jax.ShapeDtypeStruct((nodes, width), BF16),
        in_specs=[pl.BlockSpec(memory_space=pl.ANY)] * len(inputs),
        out_specs=pl.BlockSpec(memory_space=pltpu.VMEM),
        scratch_shapes=scratch,
        compiler_params=pltpu.CompilerParams(
            collective_id=0, has_side_effects=True, vmem_limit_bytes=56 << 20
        ),
    )(*inputs)


def solution(mesh):
    rows, split, full = P(("groups", "mesh"), None), P("mesh"), P()
    in_specs = (rows, split, split, rows, rows, split, split, split) + (full,) * 10
    return jax.shard_map(
        per_device, mesh=mesh, in_specs=in_specs, out_specs=rows, check_vma=False
    )
```

```python
import functools

import jax
import jax.numpy as jnp
from jax import lax
from jax.experimental import pallas as pl
from jax.experimental.pallas import tpu as pltpu
from jax.sharding import PartitionSpec as P

F32 = jnp.float32
BF16 = jnp.bfloat16
MESH = pl.DeviceIdType.MESH
GROUP = 256
CHUNK = 512
LANES = 128
DIRECT = 1
HALO_ORDER = (1, 0, 2, 3)


def dot(left, right):
    return jnp.dot(left, right, preferred_element_type=F32)


def silu(x):
    half = 0.5 * x
    return half * jnp.tanh(half) + half


def normalize(values):
    center = values - jnp.mean(values, -1, keepdims=True)
    spread = jnp.mean(center * center, -1, keepdims=True)
    return center * lax.rsqrt(spread + 1e-05)


def hot(flags):
    return jnp.where(flags, 1.0, 0.0).astype(BF16)


def prepare(state, w_first):
    width = state.shape[1]
    rows = state.astype(F32)
    mean = jnp.mean(rows, -1, keepdims=True)
    square = jnp.sum((rows - mean) * (rows - mean), -1, keepdims=True)
    top = w_first[:width, :]
    return mean, square, dot(state, top), dot(jnp.ones((8, width), BF16), top)[:1]


def update(state, prepared, gathered, w_first, w_second):
    width = state.shape[1]
    own_mean, square, product, columns = prepared
    mean = 0.5 * (own_mean + jnp.mean(gathered, -1, keepdims=True))
    low, high = own_mean - mean, gathered - mean
    spread = (
        square + width * (low * low) + jnp.sum(high * high, -1, keepdims=True)
    ) / (2 * width)
    scale = lax.rsqrt(spread + 1e-05)
    hidden = dot((high * scale).astype(BF16), w_first[width:, :])
    hidden = hidden + scale * (product - mean * columns)
    return (state.astype(F32) + dot(silu(hidden).astype(BF16), w_second[...])).astype(BF16)


def kernel(n, cap, hcap, *refs):
    hbm = refs[:18]
    out_ref = refs[18]
    (
        grid_in,
        owner,
        node_slot,
        embed,
        edges,
        senders,
        receivers,
        send_list,
        w_grid_first,
        w_grid_second,
        w_enc_first,
        w_enc_second,
        w_send,
        w_recv,
        w_edge,
        w_message,
        w_proc_first,
        w_proc_second,
    ) = vmem = refs[19:37]
    (
        latent,
        outgoing,
        arrived,
        ids_out,
        ids_in,
        pre,
        local_table,
        near_hot,
        halo_hot,
        node_hot,
        list_hot,
        halo_out,
        halo_in,
        relay_out,
        relay_in,
        relay_send,
        relay_recv,
        load_sem,
        row_send,
        row_recv,
        id_send,
        id_recv,
        halo_send,
        halo_recv,
    ) = refs[37:]
    grid_count = grid_in.shape[1]
    nodes, width = embed.shape
    edge_count = edges.shape[0]
    me = lax.axis_index("mesh")

    half, quarter, chips = n // 2, n // 4, n // 8
    q, place_in = me // quarter, me % quarter
    h = q // 2
    mine = me % half
    core = place_in % 2
    inner = (q + 1) // 2 % 2
    far_inner, far_outer, near_other = 2 - h, 3 - 3 * h, 4 * h + 1 - q
    near_inner = 1 + h
    other = lax.rem(me + half, n)
    by_class = (far_inner, far_outer, near_other, q)

    def column(j):
        return lax.rem(place_in // 2 + j % chips, chips) * 2 + j // chips

    loads = [
        pltpu.make_async_copy(source, target, load_sem.at[i])
        for i, (source, target) in enumerate(zip(hbm, vmem))
    ]
    for i in (0, 8, 1, 2, 9, 14, 4, 3, 10, 11, 7, 12, 13, 5, 6, 15, 16, 17):
        loads[i].start()
    barrier = pltpu.get_barrier_semaphore()
    for t in range(1, n):
        pl.semaphore_signal(
            barrier, inc=1, device_id={"mesh": lax.rem(me + t, n)}, device_id_type=MESH
        )

    for i in (1, 2, 0, 8, 9):
        loads[i].wait()
    block = lax.broadcasted_iota(jnp.int32, (n, 1), 0)
    kind, j = block // quarter, block % quarter
    target = jnp.where(
        kind < 2,
        jnp.where(kind == 0, far_inner, far_outer),
        jnp.where(kind == 2, near_other, q),
    )
    target = target * quarter + column(j)
    flags = jnp.where(target == owner[...], 1.0, 0.0)
    earlier = hot(
        lax.broadcasted_iota(jnp.int32, (grid_count, grid_count), 0)
        < lax.broadcasted_iota(jnp.int32, (grid_count, grid_count), 1)
    )
    rank = dot(flags.astype(BF16), earlier) + (block * cap).astype(F32)
    place = jnp.sum(flags * rank, 0, keepdims=True).astype(jnp.int32)
    slots = (flags * (node_slot[...] + 1).astype(F32)).astype(BF16)
    per_group = GROUP // cap
    lane_hot = hot(
        lax.broadcasted_iota(jnp.int32, (GROUP, grid_count), 0)
        == place % cap + mine % per_group * cap
    )
    ids = lax.dot_general(slots, lane_hot, (((1,), (1,)), ((), ())), preferred_element_type=F32)
    for t in range(n):
        ids_out[t] = ids[t : t + 1, :]

    hidden = lax.dot_general(
        grid_in[...], w_grid_first[...], (((0,), (0,)), ((), ())), preferred_element_type=F32
    )
    hidden = silu(hidden).astype(BF16)
    latent[...] = normalize(dot(hidden, w_grid_second[...])).astype(BF16)

    pl.semaphore_wait(barrier, n - 1)

    def row_copies(b, kind, slot, receiver):
        return (
            pltpu.make_async_remote_copy(
                src_ref=ids_out.at[b],
                dst_ref=ids_in.at[kind, slot],
                send_sem=id_send.at[b],
                recv_sem=id_recv.at[kind, slot],
                device_id={"mesh": receiver},
                device_id_type=MESH,
            ),
            pltpu.make_async_remote_copy(
                src_ref=outgoing.at[b],
                dst_ref=arrived.at[kind, slot],
                send_sem=row_send.at[b],
                recv_sem=row_recv.at[kind, slot],
                device_id={"mesh": receiver},
                device_id_type=MESH,
            ),
        )

    sent_rows = []
    for b in range(n):
        if b % per_group == 0:
            pack = hot(
                lax.broadcasted_iota(jnp.int32, (GROUP, grid_count), 0) + b * cap == place
            )
            packed = dot(pack, latent[...]).astype(BF16)
            outgoing[b : b + per_group] = packed.reshape(per_group, cap, width)
        kind, j = b // quarter, b % quarter
        col = column(j)
        if kind == 0:
            receiver = near_inner * quarter + col
        elif kind == 1:
            receiver = jnp.where(
                jnp.int32(j // chips) < DIRECT, far_outer * quarter, near_inner * quarter
            ) + col
        else:
            receiver = by_class[kind] * quarter + col
        slot_kind = min(kind, 2)
        copies = row_copies(b, slot_kind, mine, receiver)
        if j % chips == 0 and (kind != 2) and not (kind == 1 and j // chips < DIRECT):
            own = (core == j // chips) & (True if kind == 3 else inner == 1)
            sent_rows.append((copies, own))

            @pl.when(own)
            def _():
                ids_in[slot_kind, mine] = ids_out[b]
                arrived[slot_kind, mine] = outgoing[b]

            @pl.when(jnp.logical_not(own))
            def _():
                copies[0].start()
                copies[1].start()
        else:
            sent_rows.append((copies, None))
            copies[0].start()
            copies[1].start()

    loads[14].wait()
    loads[4].wait()
    for chunk in range(edge_count // CHUNK):
        rows = pl.ds(chunk * CHUNK, CHUNK)
        pre[rows, :] = dot(edges[rows, :], w_edge[...])

    loads[5].wait()
    loads[6].wait()
    loads[7].wait()
    sender_columns = jnp.transpose(senders[...])
    receiver_columns = jnp.transpose(receivers[...])
    list_columns = jnp.transpose(send_list[...])
    near_iota = lax.broadcasted_iota(jnp.int32, (LANES, nodes), 1)
    lane = lax.broadcasted_iota(jnp.int32, (1, n * hcap), 1)
    halo_place = nodes + lax.rem(lane + h * (half * hcap), n * hcap)
    node_iota = lax.broadcasted_iota(jnp.int32, (nodes, LANES), 0)
    for part in range(edge_count // LANES):
        rows = pl.ds(part * LANES, LANES)
        sender = sender_columns[:, part : part + 1]
        receiver = receiver_columns[:, part : part + 1]
        near_hot[rows, :nodes] = hot(sender == near_iota)
        near_hot[rows, nodes:] = hot(receiver == near_iota)
        halo_hot[rows, :] = hot(sender == halo_place)
        node_hot[:, part * LANES : (part + 1) * LANES] = hot(
            receivers[part : part + 1, :] == node_iota
        )
    list_iota = lax.broadcasted_iota(jnp.int32, (hcap, nodes), 1)
    for p in range(n):
        list_hot[p * hcap : (p + 1) * hcap, :] = hot(list_columns[:, p : p + 1] == list_iota)

    for i in (3, 10, 11, 12, 13):
        loads[i].wait()
    prepared = prepare(embed[...], w_enc_first)
    slot_iota = lax.broadcasted_iota(jnp.int32, (nodes, GROUP), 0).astype(F32) + 1.0

    def await_rows(kind, slot):
        copies = row_copies(0, kind, slot, other)
        copies[0].wait_recv()
        copies[1].wait_recv()

    def collect(kind, all_remote):
        total = jnp.zeros((nodes, width), F32)
        for first in range(0, half, per_group):
            named = jnp.zeros((1, GROUP), F32)
            for s in range(first, first + per_group):

                @pl.when(all_remote | (mine != s))
                def _():
                    await_rows(kind, s)

                named = named + ids_in[kind, s]
            total = total + dot(
                hot(slot_iota == named),
                arrived[kind, first : first + per_group].reshape(GROUP, width),
            )
        return total

    def relay(i, receiver):
        return pltpu.make_async_remote_copy(
            src_ref=relay_out.at[i],
            dst_ref=relay_in,
            send_sem=relay_send.at[i],
            recv_sem=relay_recv.at[0],
            device_id={"mesh": receiver},
            device_id_type=MESH,
        )

    relays = (relay(0, far_inner * quarter + place_in), relay(1, far_outer * quarter + place_in))
    direct = jnp.where(core < DIRECT, 1, 0)

    @pl.when(inner == 1)
    def _():
        relay_out[0] = collect(0, False).astype(BF16)
        relays[0].start()

    @pl.when(inner * (1 - direct) == 1)
    def _():
        relay_out[1] = collect(1, False).astype(BF16)
        relays[1].start()

    @pl.when((1 - inner) * direct == 1)
    def _():
        relay_in[...] = collect(1, True).astype(BF16)

    gathered = collect(2, False)

    @pl.when((1 - inner) * direct == 0)
    def _():
        relays[0].wait_recv()

    gathered = gathered + relay_in[...].astype(F32)

    state = update(embed[...], prepared, gathered, w_enc_first, w_enc_second)
    sent = dot(state, w_send[...]).astype(BF16)
    inner_rows = half * hcap

    def list_rows(side):
        rows = dot(list_hot[pl.ds(side * inner_rows, inner_rows), :], sent)
        halo_out[pl.ds(side * half, half)] = rows.astype(BF16).reshape(half, hcap, width)

    list_rows(1 - h)

    def halo_copy(b, slot, receiver):
        return pltpu.make_async_remote_copy(
            src_ref=halo_out.at[receiver],
            dst_ref=halo_in.at[slot],
            send_sem=halo_send.at[b],
            recv_sem=halo_recv.at[slot],
            device_id={"mesh": receiver},
            device_id_type=MESH,
        )

    sent_halos = []
    for b in range(n):
        if b == half:
            list_rows(h)
        kind, j = HALO_ORDER[b // quarter], b % quarter
        receiver = by_class[kind] * quarter + column(j)
        copy = halo_copy(b, mine + half if kind < 2 else mine, receiver)
        if kind == 3 and j % chips == 0:
            own = core == j // chips
            sent_halos.append((copy, own))

            @pl.when(jnp.logical_not(own))
            def _():
                copy.start()
        else:
            sent_halos.append((copy, None))
            copy.start()
    halo_in[mine] = halo_out[me]
    local_table[:nodes, :] = sent
    local_table[nodes:, :] = dot(state, w_recv[...]).astype(BF16)
    for chunk in range(edge_count // CHUNK):
        rows = pl.ds(chunk * CHUNK, CHUNK)
        pre[rows, :] += dot(near_hot[rows, :], local_table[...])

    for i in (15, 16, 17):
        loads[i].wait()
    prepared = prepare(state, w_proc_first)
    for s in range(half):

        @pl.when(mine != s)
        def _():
            halo_copy(0, s, other).wait_recv()

    halo = halo_in[:half].reshape(inner_rows, width)
    for chunk in range(edge_count // CHUNK):
        rows = pl.ds(chunk * CHUNK, CHUNK)
        pre[rows, :] += dot(halo_hot[rows, :inner_rows], halo)
    for s in range(half, n):
        halo_copy(0, s, other).wait_recv()
    halo = halo_in[half:].reshape(inner_rows, width)
    summed = jnp.zeros((nodes, width), F32)
    for chunk in range(edge_count // CHUNK):
        rows = pl.ds(chunk * CHUNK, CHUNK)
        edge_pre = pre[rows, :] + dot(halo_hot[rows, inner_rows:], halo)
        summed = summed + dot(
            node_hot[:, chunk * CHUNK : (chunk + 1) * CHUNK], silu(edge_pre).astype(BF16)
        )
    node_sum = dot(summed.astype(BF16), w_message[...])
    out_ref[...] = update(state, prepared, node_sum, w_proc_first, w_proc_second)

    @pl.when(inner == 1)
    def _():
        relays[0].wait_send()

    @pl.when(inner * (1 - direct) == 1)
    def _():
        relays[1].wait_send()

    for copies, own in sent_rows:
        if own is None:
            copies[0].wait_send()
            copies[1].wait_send()
        else:

            @pl.when(jnp.logical_not(own))
            def _():
                copies[0].wait_send()
                copies[1].wait_send()

    for copy, own in sent_halos:
        if own is None:
            copy.wait_send()
        else:

            @pl.when(jnp.logical_not(own))
            def _():
                copy.wait_send()


def per_device(
    grid_in, owner, node_slot, mesh_embed, edge_latent, senders, receivers, send_list, *weights
):
    n = lax.axis_size("mesh")
    grid_count = grid_in.shape[0]
    nodes, width = mesh_embed.shape
    edge_count = edge_latent.shape[0]
    list_size = send_list.shape[1]
    cap = max(16, 2 * grid_count // n)
    hcap = max(16, list_size)
    if hcap != list_size:
        beyond = jnp.maximum(senders - nodes, 0)
        moved = nodes + beyond // list_size * hcap + beyond % list_size
        senders = jnp.where(senders < nodes, senders, moved)
        send_list = jnp.pad(send_list, ((0, 0), (0, hcap - list_size)))
    inputs = (
        grid_in.T,
        owner.reshape(1, grid_count),
        node_slot.reshape(1, grid_count),
        mesh_embed,
        edge_latent,
        senders.reshape(edge_count // LANES, LANES),
        receivers.reshape(edge_count // LANES, LANES),
        send_list,
    ) + weights
    dma = pltpu.SemaphoreType.DMA
    scratch = [pltpu.VMEM(x.shape, x.dtype) for x in inputs] + [
        pltpu.VMEM((grid_count, width), BF16),
        pltpu.VMEM((n, cap, width), BF16),
        pltpu.VMEM((3, n // 2, cap, width), BF16),
        pltpu.VMEM((n, 1, GROUP), F32),
        pltpu.VMEM((3, n // 2, 1, GROUP), F32),
        pltpu.VMEM((edge_count, width), F32),
        pltpu.VMEM((2 * nodes, width), BF16),
        pltpu.VMEM((edge_count, 2 * nodes), BF16),
        pltpu.VMEM((edge_count, n * hcap), BF16),
        pltpu.VMEM((nodes, edge_count), BF16),
        pltpu.VMEM((n * hcap, nodes), BF16),
        pltpu.VMEM((n, hcap, width), BF16),
        pltpu.VMEM((n, hcap, width), BF16),
        pltpu.VMEM((2, nodes, width), BF16),
        pltpu.VMEM((nodes, width), BF16),
        dma((2,)),
        dma((1,)),
        dma((len(inputs),)),
        dma((n,)),
        dma((3, n // 2)),
        dma((n,)),
        dma((3, n // 2)),
        dma((n,)),
        dma((n,)),
    ]
    return pl.pallas_call(
        functools.partial(kernel, n, cap, hcap),
        out_shape=jax.ShapeDtypeStruct((nodes, width), BF16),
        in_specs=[pl.BlockSpec(memory_space=pl.ANY)] * len(inputs),
        out_specs=pl.BlockSpec(memory_space=pltpu.VMEM),
        scratch_shapes=scratch,
        compiler_params=pltpu.CompilerParams(
            collective_id=0, has_side_effects=True, vmem_limit_bytes=56 << 20
        ),
    )(*inputs)


def solution(mesh):
    rows, split, full = P(("groups", "mesh"), None), P("mesh"), P()
    in_specs = (rows, split, split, rows, rows, split, split, split) + (full,) * 10
    return jax.shard_map(
        per_device, mesh=mesh, in_specs=in_specs, out_specs=rows, check_vma=False
    )
```

```python
import functools

import jax
import jax.numpy as jnp
from jax import lax
from jax.experimental import pallas as pl
from jax.experimental.pallas import tpu as pltpu
from jax.sharding import PartitionSpec as P

F32 = jnp.float32
BF16 = jnp.bfloat16
MESH = pl.DeviceIdType.MESH
GROUP = 256
CHUNK = 512
LANES = 128
DIRECT = 0
ROW_ORDER = ((0, 0), (0, 1), (1, 0), (1, 1), (2, 1), (2, 0), (3, 0), (3, 1))
HALO_ORDER = ((1, 0), (1, 1), (0, 0), (0, 1), (2, 0), (2, 1), (3, 0), (3, 1))


def dot(left, right):
    return jnp.dot(left, right, preferred_element_type=F32)


def silu(x):
    half = 0.5 * x
    return half * jnp.tanh(half) + half


def normalize(values):
    center = values - jnp.mean(values, -1, keepdims=True)
    spread = jnp.mean(center * center, -1, keepdims=True)
    return center * lax.rsqrt(spread + 1e-05)


def hot(flags):
    return jnp.where(flags, 1.0, 0.0).astype(BF16)


def prepare(state, w_first):
    width = state.shape[1]
    rows = state.astype(F32)
    mean = jnp.mean(rows, -1, keepdims=True)
    square = jnp.sum((rows - mean) * (rows - mean), -1, keepdims=True)
    top = w_first[:width, :]
    return mean, square, dot(state, top), dot(jnp.ones((8, width), BF16), top)[:1]


def update(state, prepared, gathered, w_first, w_second):
    width = state.shape[1]
    own_mean, square, product, columns = prepared
    mean = 0.5 * (own_mean + jnp.mean(gathered, -1, keepdims=True))
    low, high = own_mean - mean, gathered - mean
    spread = (
        square + width * (low * low) + jnp.sum(high * high, -1, keepdims=True)
    ) / (2 * width)
    scale = lax.rsqrt(spread + 1e-05)
    hidden = dot((high * scale).astype(BF16), w_first[width:, :])
    hidden = hidden + scale * (product - mean * columns)
    return (state.astype(F32) + dot(silu(hidden).astype(BF16), w_second[...])).astype(BF16)


def kernel(n, cap, hcap, *refs):
    hbm = refs[:18]
    out_ref = refs[18]
    (
        grid_in,
        owner,
        node_slot,
        embed,
        edges,
        senders,
        receivers,
        send_list,
        w_grid_first,
        w_grid_second,
        w_enc_first,
        w_enc_second,
        w_send,
        w_recv,
        w_edge,
        w_message,
        w_proc_first,
        w_proc_second,
    ) = vmem = refs[19:37]
    (
        latent,
        outgoing,
        arrived,
        ids_out,
        ids_in,
        pre,
        local_table,
        near_hot,
        halo_hot,
        node_hot,
        list_hot,
        halo_out,
        halo_in,
        relay_out,
        relay_in,
        relay_send,
        relay_recv,
        load_sem,
        row_send,
        row_recv,
        id_send,
        id_recv,
        halo_send,
        halo_recv,
    ) = refs[37:]
    grid_count = grid_in.shape[1]
    nodes, width = embed.shape
    edge_count = edges.shape[0]
    me = lax.axis_index("mesh")

    half, quarter, chips = n // 2, n // 4, n // 8
    q, place_in = me // quarter, me % quarter
    h = q // 2
    mine = me % half
    core = place_in % 2
    inner = (q + 1) // 2 % 2
    far_inner, far_outer, near_other = 2 - h, 3 - 3 * h, 4 * h + 1 - q
    near_inner = 1 + h
    other = lax.rem(me + half, n)
    by_class = (far_inner, far_outer, near_other, q)

    def column(j, side):
        return lax.rem(place_in // 2 + j % chips, chips) * 2 + side

    loads = [
        pltpu.make_async_copy(source, target, load_sem.at[i])
        for i, (source, target) in enumerate(zip(hbm, vmem))
    ]
    for i in (0, 8, 1, 2, 9, 14, 4, 3, 10, 11, 7, 12, 13, 5, 6, 15, 16, 17):
        loads[i].start()
    barrier = pltpu.get_barrier_semaphore()
    for t in range(1, n):
        pl.semaphore_signal(
            barrier, inc=1, device_id={"mesh": lax.rem(me + t, n)}, device_id_type=MESH
        )

    for i in (1, 2, 0, 8, 9):
        loads[i].wait()
    block = lax.broadcasted_iota(jnp.int32, (n, 1), 0)
    turn = block // chips
    target = column(block, 0)
    for i, (kind, side) in enumerate(ROW_ORDER):
        target = target + jnp.where(turn == i, by_class[kind] * quarter + side, 0)
    flags = jnp.where(target == owner[...], 1.0, 0.0)
    earlier = hot(
        lax.broadcasted_iota(jnp.int32, (grid_count, grid_count), 0)
        < lax.broadcasted_iota(jnp.int32, (grid_count, grid_count), 1)
    )
    rank = dot(flags.astype(BF16), earlier) + (block * cap).astype(F32)
    place = jnp.sum(flags * rank, 0, keepdims=True).astype(jnp.int32)
    slots = (flags * (node_slot[...] + 1).astype(F32)).astype(BF16)
    per_group = GROUP // cap
    lane_hot = hot(
        lax.broadcasted_iota(jnp.int32, (GROUP, grid_count), 0)
        == place % cap + mine % per_group * cap
    )
    ids = lax.dot_general(slots, lane_hot, (((1,), (1,)), ((), ())), preferred_element_type=F32)
    for t in range(n):
        ids_out[t] = ids[t : t + 1, :]

    hidden = lax.dot_general(
        grid_in[...], w_grid_first[...], (((0,), (0,)), ((), ())), preferred_element_type=F32
    )
    hidden = silu(hidden).astype(BF16)
    latent[...] = normalize(dot(hidden, w_grid_second[...])).astype(BF16)

    pl.semaphore_wait(barrier, n - 1)

    def row_copies(b, kind, slot, receiver):
        return (
            pltpu.make_async_remote_copy(
                src_ref=ids_out.at[b],
                dst_ref=ids_in.at[kind, slot],
                send_sem=id_send.at[b],
                recv_sem=id_recv.at[kind, slot],
                device_id={"mesh": receiver},
                device_id_type=MESH,
            ),
            pltpu.make_async_remote_copy(
                src_ref=outgoing.at[b],
                dst_ref=arrived.at[kind, slot],
                send_sem=row_send.at[b],
                recv_sem=row_recv.at[kind, slot],
                device_id={"mesh": receiver},
                device_id_type=MESH,
            ),
        )

    sent_rows = []
    for b in range(n):
        if b % per_group == 0:
            pack = hot(
                lax.broadcasted_iota(jnp.int32, (GROUP, grid_count), 0) + b * cap == place
            )
            packed = dot(pack, latent[...]).astype(BF16)
            outgoing[b : b + per_group] = packed.reshape(per_group, cap, width)
        kind, side = ROW_ORDER[b // chips]
        col = column(b, side)
        if kind == 0:
            receiver = near_inner * quarter + col
        elif kind == 1:
            receiver = (far_outer if side == DIRECT else near_inner) * quarter + col
        else:
            receiver = by_class[kind] * quarter + col
        slot_kind = min(kind, 2)
        copies = row_copies(b, slot_kind, mine, receiver)
        if b % chips == 0 and kind != 2 and (kind, side) != (1, DIRECT):
            own = (core == side) & (True if kind == 3 else inner == 1)
            sent_rows.append((copies, own))

            @pl.when(own)
            def _():
                ids_in[slot_kind, mine] = ids_out[b]
                arrived[slot_kind, mine] = outgoing[b]

            @pl.when(jnp.logical_not(own))
            def _():
                copies[0].start()
                copies[1].start()
        else:
            sent_rows.append((copies, None))
            copies[0].start()
            copies[1].start()

    loads[14].wait()
    loads[4].wait()
    for chunk in range(edge_count // CHUNK):
        rows = pl.ds(chunk * CHUNK, CHUNK)
        pre[rows, :] = dot(edges[rows, :], w_edge[...])

    loads[5].wait()
    loads[6].wait()
    loads[7].wait()
    sender_columns = jnp.transpose(senders[...])
    receiver_columns = jnp.transpose(receivers[...])
    list_columns = jnp.transpose(send_list[...])
    near_iota = lax.broadcasted_iota(jnp.int32, (LANES, nodes), 1)
    lane = lax.broadcasted_iota(jnp.int32, (1, n * hcap), 1)
    halo_place = nodes + lax.rem(lane + h * (half * hcap), n * hcap)
    node_iota = lax.broadcasted_iota(jnp.int32, (nodes, LANES), 0)
    for part in range(edge_count // LANES):
        rows = pl.ds(part * LANES, LANES)
        sender = sender_columns[:, part : part + 1]
        receiver = receiver_columns[:, part : part + 1]
        near_hot[rows, :nodes] = hot(sender == near_iota)
        near_hot[rows, nodes:] = hot(receiver == near_iota)
        halo_hot[rows, :] = hot(sender == halo_place)
        node_hot[:, part * LANES : (part + 1) * LANES] = hot(
            receivers[part : part + 1, :] == node_iota
        )
    list_iota = lax.broadcasted_iota(jnp.int32, (hcap, nodes), 1)
    for p in range(n):
        list_hot[p * hcap : (p + 1) * hcap, :] = hot(list_columns[:, p : p + 1] == list_iota)

    for i in (3, 10, 11, 12, 13):
        loads[i].wait()
    prepared = prepare(embed[...], w_enc_first)
    slot_iota = lax.broadcasted_iota(jnp.int32, (nodes, GROUP), 0).astype(F32) + 1.0

    def await_rows(kind, slot):
        copies = row_copies(0, kind, slot, other)
        copies[0].wait_recv()
        copies[1].wait_recv()

    def collect(kind, all_remote):
        total = jnp.zeros((nodes, width), F32)
        for first in range(0, half, per_group):
            named = jnp.zeros((1, GROUP), F32)
            for s in range(first, first + per_group):

                @pl.when(all_remote | (mine != s))
                def _():
                    await_rows(kind, s)

                named = named + ids_in[kind, s]
            total = total + dot(
                hot(slot_iota == named),
                arrived[kind, first : first + per_group].reshape(GROUP, width),
            )
        return total

    def relay(i, receiver):
        return pltpu.make_async_remote_copy(
            src_ref=relay_out.at[i],
            dst_ref=relay_in,
            send_sem=relay_send.at[i],
            recv_sem=relay_recv.at[0],
            device_id={"mesh": receiver},
            device_id_type=MESH,
        )

    relays = (relay(0, far_inner * quarter + place_in), relay(1, far_outer * quarter + place_in))
    direct = jnp.where(core == DIRECT, 1, 0)

    @pl.when(inner == 1)
    def _():
        relay_out[0] = collect(0, False).astype(BF16)
        relays[0].start()

    @pl.when(inner * (1 - direct) == 1)
    def _():
        relay_out[1] = collect(1, False).astype(BF16)
        relays[1].start()

    @pl.when((1 - inner) * direct == 1)
    def _():
        relay_in[...] = collect(1, True).astype(BF16)

    gathered = collect(2, False)

    @pl.when((1 - inner) * direct == 0)
    def _():
        relays[0].wait_recv()

    gathered = gathered + relay_in[...].astype(F32)

    state = update(embed[...], prepared, gathered, w_enc_first, w_enc_second)
    sent = dot(state, w_send[...]).astype(BF16)
    inner_rows = half * hcap

    def list_rows(side):
        rows = dot(list_hot[pl.ds(side * inner_rows, inner_rows), :], sent)
        halo_out[pl.ds(side * half, half)] = rows.astype(BF16).reshape(half, hcap, width)

    list_rows(1 - h)

    def halo_copy(b, slot, receiver):
        return pltpu.make_async_remote_copy(
            src_ref=halo_out.at[receiver],
            dst_ref=halo_in.at[slot],
            send_sem=halo_send.at[b],
            recv_sem=halo_recv.at[slot],
            device_id={"mesh": receiver},
            device_id_type=MESH,
        )

    sent_halos = []
    for b in range(n):
        if b == half:
            list_rows(h)
        kind, side = HALO_ORDER[b // chips]
        receiver = by_class[kind] * quarter + column(b, side)
        copy = halo_copy(b, mine + half if kind < 2 else mine, receiver)
        if kind == 3 and b % chips == 0:
            own = core == side
            sent_halos.append((copy, own))

            @pl.when(jnp.logical_not(own))
            def _():
                copy.start()
        else:
            sent_halos.append((copy, None))
            copy.start()
    halo_in[mine] = halo_out[me]
    local_table[:nodes, :] = sent
    local_table[nodes:, :] = dot(state, w_recv[...]).astype(BF16)
    for chunk in range(edge_count // CHUNK):
        rows = pl.ds(chunk * CHUNK, CHUNK)
        pre[rows, :] += dot(near_hot[rows, :], local_table[...])

    for i in (15, 16, 17):
        loads[i].wait()
    prepared = prepare(state, w_proc_first)
    for s in range(half):

        @pl.when(mine != s)
        def _():
            halo_copy(0, s, other).wait_recv()

    halo = halo_in[:half].reshape(inner_rows, width)
    for chunk in range(edge_count // CHUNK):
        rows = pl.ds(chunk * CHUNK, CHUNK)
        pre[rows, :] += dot(halo_hot[rows, :inner_rows], halo)
    for s in range(half, n):
        halo_copy(0, s, other).wait_recv()
    halo = halo_in[half:].reshape(inner_rows, width)
    summed = jnp.zeros((nodes, width), F32)
    for chunk in range(edge_count // CHUNK):
        rows = pl.ds(chunk * CHUNK, CHUNK)
        edge_pre = pre[rows, :] + dot(halo_hot[rows, inner_rows:], halo)
        summed = summed + dot(
            node_hot[:, chunk * CHUNK : (chunk + 1) * CHUNK], silu(edge_pre).astype(BF16)
        )
    node_sum = dot(summed.astype(BF16), w_message[...])
    out_ref[...] = update(state, prepared, node_sum, w_proc_first, w_proc_second)

    @pl.when(inner == 1)
    def _():
        relays[0].wait_send()

    @pl.when(inner * (1 - direct) == 1)
    def _():
        relays[1].wait_send()

    for copies, own in sent_rows:
        if own is None:
            copies[0].wait_send()
            copies[1].wait_send()
        else:

            @pl.when(jnp.logical_not(own))
            def _():
                copies[0].wait_send()
                copies[1].wait_send()

    for copy, own in sent_halos:
        if own is None:
            copy.wait_send()
        else:

            @pl.when(jnp.logical_not(own))
            def _():
                copy.wait_send()


def per_device(
    grid_in, owner, node_slot, mesh_embed, edge_latent, senders, receivers, send_list, *weights
):
    n = lax.axis_size("mesh")
    grid_count = grid_in.shape[0]
    nodes, width = mesh_embed.shape
    edge_count = edge_latent.shape[0]
    list_size = send_list.shape[1]
    cap = max(16, 2 * grid_count // n)
    hcap = max(16, list_size)
    if hcap != list_size:
        beyond = jnp.maximum(senders - nodes, 0)
        moved = nodes + beyond // list_size * hcap + beyond % list_size
        senders = jnp.where(senders < nodes, senders, moved)
        send_list = jnp.pad(send_list, ((0, 0), (0, hcap - list_size)))
    inputs = (
        grid_in.T,
        owner.reshape(1, grid_count),
        node_slot.reshape(1, grid_count),
        mesh_embed,
        edge_latent,
        senders.reshape(edge_count // LANES, LANES),
        receivers.reshape(edge_count // LANES, LANES),
        send_list,
    ) + weights
    dma = pltpu.SemaphoreType.DMA
    scratch = [pltpu.VMEM(x.shape, x.dtype) for x in inputs] + [
        pltpu.VMEM((grid_count, width), BF16),
        pltpu.VMEM((n, cap, width), BF16),
        pltpu.VMEM((3, n // 2, cap, width), BF16),
        pltpu.VMEM((n, 1, GROUP), F32),
        pltpu.VMEM((3, n // 2, 1, GROUP), F32),
        pltpu.VMEM((edge_count, width), F32),
        pltpu.VMEM((2 * nodes, width), BF16),
        pltpu.VMEM((edge_count, 2 * nodes), BF16),
        pltpu.VMEM((edge_count, n * hcap), BF16),
        pltpu.VMEM((nodes, edge_count), BF16),
        pltpu.VMEM((n * hcap, nodes), BF16),
        pltpu.VMEM((n, hcap, width), BF16),
        pltpu.VMEM((n, hcap, width), BF16),
        pltpu.VMEM((2, nodes, width), BF16),
        pltpu.VMEM((nodes, width), BF16),
        dma((2,)),
        dma((1,)),
        dma((len(inputs),)),
        dma((n,)),
        dma((3, n // 2)),
        dma((n,)),
        dma((3, n // 2)),
        dma((n,)),
        dma((n,)),
    ]
    return pl.pallas_call(
        functools.partial(kernel, n, cap, hcap),
        out_shape=jax.ShapeDtypeStruct((nodes, width), BF16),
        in_specs=[pl.BlockSpec(memory_space=pl.ANY)] * len(inputs),
        out_specs=pl.BlockSpec(memory_space=pltpu.VMEM),
        scratch_shapes=scratch,
        compiler_params=pltpu.CompilerParams(
            collective_id=0, has_side_effects=True, vmem_limit_bytes=56 << 20
        ),
    )(*inputs)


def solution(mesh):
    rows, split, full = P(("groups", "mesh"), None), P("mesh"), P()
    in_specs = (rows, split, split, rows, rows, split, split, split) + (full,) * 10
    return jax.shard_map(
        per_device, mesh=mesh, in_specs=in_specs, out_specs=rows, check_vma=False
    )
```

```python
import functools

import jax
import jax.numpy as jnp
from jax import lax
from jax.experimental import pallas as pl
from jax.experimental.pallas import tpu as pltpu
from jax.sharding import PartitionSpec as P

F32 = jnp.float32
BF16 = jnp.bfloat16
MESH = pl.DeviceIdType.MESH
GROUP = 256
CHUNK = 1024
LANES = 128
DIRECT = 0
ROW_ORDER = ((0, 1), (0, 0), (1, 0), (1, 1), (2, 1), (2, 0), (3, 1), (3, 0))
HALO_ORDER = ((1, 0), (1, 1), (0, 0), (0, 1), (2, 0), (2, 1), (3, 0), (3, 1))


def dot(left, right):
    return jnp.dot(left, right, preferred_element_type=F32)


def silu(x):
    half = 0.5 * x
    return half * jnp.tanh(half) + half


def normalize(values):
    center = values - jnp.mean(values, -1, keepdims=True)
    spread = jnp.mean(center * center, -1, keepdims=True)
    return center * lax.rsqrt(spread + 1e-05)


def hot(flags):
    return jnp.where(flags, 1.0, 0.0).astype(BF16)


def prepare(state, w_first):
    width = state.shape[1]
    rows = state.astype(F32)
    mean = jnp.mean(rows, -1, keepdims=True)
    square = jnp.sum((rows - mean) * (rows - mean), -1, keepdims=True)
    top = w_first[:width, :]
    return mean, square, dot(state, top), dot(jnp.ones((8, width), BF16), top)[:1]


def update(state, prepared, gathered, w_first, w_second):
    width = state.shape[1]
    own_mean, square, product, columns = prepared
    mean = 0.5 * (own_mean + jnp.mean(gathered, -1, keepdims=True))
    low, high = own_mean - mean, gathered - mean
    spread = (
        square + width * (low * low) + jnp.sum(high * high, -1, keepdims=True)
    ) / (2 * width)
    scale = lax.rsqrt(spread + 1e-05)
    hidden = dot((high * scale).astype(BF16), w_first[width:, :])
    hidden = hidden + scale * (product - mean * columns)
    return (state.astype(F32) + dot(silu(hidden).astype(BF16), w_second[...])).astype(BF16)


def kernel(n, cap, hcap, *refs):
    hbm = refs[:18]
    out_ref = refs[18]
    (
        grid_in,
        owner,
        node_slot,
        embed,
        edges,
        senders,
        receivers,
        send_list,
        w_grid_first,
        w_grid_second,
        w_enc_first,
        w_enc_second,
        w_send,
        w_recv,
        w_edge,
        w_message,
        w_proc_first,
        w_proc_second,
    ) = vmem = refs[19:37]
    (
        latent,
        outgoing,
        arrived,
        ids_out,
        ids_in,
        pre,
        local_table,
        near_hot,
        halo_hot,
        node_hot,
        list_hot,
        halo_out,
        halo_in,
        relay_out,
        relay_in,
        relay_send,
        relay_recv,
        load_sem,
        row_send,
        row_recv,
        id_send,
        id_recv,
        halo_send,
        halo_recv,
    ) = refs[37:]
    grid_count = grid_in.shape[1]
    nodes, width = embed.shape
    edge_count = edges.shape[0]
    me = lax.axis_index("mesh")

    half, quarter, chips = n // 2, n // 4, n // 8
    q, place_in = me // quarter, me % quarter
    h = q // 2
    mine = me % half
    core = place_in % 2
    inner = (q + 1) // 2 % 2
    far_inner, far_outer, near_other = 2 - h, 3 - 3 * h, 4 * h + 1 - q
    near_inner = 1 + h
    other = lax.rem(me + half, n)
    by_class = (far_inner, far_outer, near_other, q)

    def column(j, side, first=0):
        return lax.rem(place_in // 2 + (j + first) % chips, chips) * 2 + side

    loads = [
        pltpu.make_async_copy(source, target, load_sem.at[i])
        for i, (source, target) in enumerate(zip(hbm, vmem))
    ]
    for i in (0, 8, 1, 2, 9, 14, 4, 3, 10, 11, 7, 12, 13, 5, 6, 15, 16, 17):
        loads[i].start()
    barrier = pltpu.get_barrier_semaphore()
    for t in range(1, n):
        pl.semaphore_signal(
            barrier, inc=1, device_id={"mesh": lax.rem(me + t, n)}, device_id_type=MESH
        )

    for i in (1, 2, 0, 8, 9):
        loads[i].wait()
    block = lax.broadcasted_iota(jnp.int32, (n, 1), 0)
    turn = block // chips
    target = column(block, 0, 1)
    for i, (kind, side) in enumerate(ROW_ORDER):
        target = target + jnp.where(turn == i, by_class[kind] * quarter + side, 0)
    flags = jnp.where(target == owner[...], 1.0, 0.0)
    earlier = hot(
        lax.broadcasted_iota(jnp.int32, (grid_count, grid_count), 0)
        < lax.broadcasted_iota(jnp.int32, (grid_count, grid_count), 1)
    )
    rank = dot(flags.astype(BF16), earlier) + (block * cap).astype(F32)
    place = jnp.sum(flags * rank, 0, keepdims=True).astype(jnp.int32)
    slots = (flags * (node_slot[...] + 1).astype(F32)).astype(BF16)
    per_group = GROUP // cap
    lane_hot = hot(
        lax.broadcasted_iota(jnp.int32, (GROUP, grid_count), 0)
        == place % cap + mine % per_group * cap
    )
    ids = lax.dot_general(slots, lane_hot, (((1,), (1,)), ((), ())), preferred_element_type=F32)
    for t in range(n):
        ids_out[t] = ids[t : t + 1, :]

    hidden = lax.dot_general(
        grid_in[...], w_grid_first[...], (((0,), (0,)), ((), ())), preferred_element_type=F32
    )
    hidden = silu(hidden).astype(BF16)
    latent[...] = normalize(dot(hidden, w_grid_second[...])).astype(BF16)

    pl.semaphore_wait(barrier, n - 1)

    def row_copies(b, kind, slot, receiver):
        return (
            pltpu.make_async_remote_copy(
                src_ref=ids_out.at[b],
                dst_ref=ids_in.at[kind, slot],
                send_sem=id_send.at[b],
                recv_sem=id_recv.at[kind, slot],
                device_id={"mesh": receiver},
                device_id_type=MESH,
            ),
            pltpu.make_async_remote_copy(
                src_ref=outgoing.at[b],
                dst_ref=arrived.at[kind, slot],
                send_sem=row_send.at[b],
                recv_sem=row_recv.at[kind, slot],
                device_id={"mesh": receiver},
                device_id_type=MESH,
            ),
        )

    sent_rows = []
    for b in range(n):
        if b % per_group == 0:
            pack = hot(
                lax.broadcasted_iota(jnp.int32, (GROUP, grid_count), 0) + b * cap == place
            )
            packed = dot(pack, latent[...]).astype(BF16)
            outgoing[b : b + per_group] = packed.reshape(per_group, cap, width)
        kind, side = ROW_ORDER[b // chips]
        col = column(b, side, 1)
        if kind == 0:
            receiver = near_inner * quarter + col
        elif kind == 1:
            receiver = (far_outer if side == DIRECT else near_inner) * quarter + col
        else:
            receiver = by_class[kind] * quarter + col
        slot_kind = min(kind, 2)
        copies = row_copies(b, slot_kind, mine, receiver)
        if (b + 1) % chips == 0 and kind != 2 and (kind, side) != (1, DIRECT):
            own = (core == side) & (True if kind == 3 else inner == 1)
            sent_rows.append((copies, own))

            @pl.when(own)
            def _():
                ids_in[slot_kind, mine] = ids_out[b]
                arrived[slot_kind, mine] = outgoing[b]

            @pl.when(jnp.logical_not(own))
            def _():
                copies[0].start()
                copies[1].start()
        else:
            sent_rows.append((copies, None))
            copies[0].start()
            copies[1].start()

    loads[14].wait()
    loads[4].wait()
    for chunk in range(edge_count // CHUNK):
        rows = pl.ds(chunk * CHUNK, CHUNK)
        pre[rows, :] = dot(edges[rows, :], w_edge[...])

    loads[5].wait()
    loads[6].wait()
    loads[7].wait()
    sender_columns = jnp.transpose(senders[...])
    receiver_columns = jnp.transpose(receivers[...])
    list_columns = jnp.transpose(send_list[...])
    near_iota = lax.broadcasted_iota(jnp.int32, (LANES, nodes), 1)
    lane = lax.broadcasted_iota(jnp.int32, (1, n * hcap), 1)
    halo_place = nodes + lax.rem(lane + h * (half * hcap), n * hcap)
    node_iota = lax.broadcasted_iota(jnp.int32, (nodes, LANES), 0)
    for part in range(edge_count // LANES):
        rows = pl.ds(part * LANES, LANES)
        sender = sender_columns[:, part : part + 1]
        receiver = receiver_columns[:, part : part + 1]
        near_hot[rows, :nodes] = hot(sender == near_iota)
        near_hot[rows, nodes:] = hot(receiver == near_iota)
        halo_hot[rows, :] = hot(sender == halo_place)
        node_hot[:, part * LANES : (part + 1) * LANES] = hot(
            receivers[part : part + 1, :] == node_iota
        )
    list_iota = lax.broadcasted_iota(jnp.int32, (hcap, nodes), 1)
    for p in range(n):
        list_hot[p * hcap : (p + 1) * hcap, :] = hot(list_columns[:, p : p + 1] == list_iota)

    for i in (3, 10, 11, 12, 13):
        loads[i].wait()
    prepared = prepare(embed[...], w_enc_first)
    slot_iota = lax.broadcasted_iota(jnp.int32, (nodes, GROUP), 0).astype(F32) + 1.0

    def await_rows(kind, slot):
        copies = row_copies(0, kind, slot, other)
        copies[0].wait_recv()
        copies[1].wait_recv()

    def collect(kind, all_remote):
        total = jnp.zeros((nodes, width), F32)
        for first in range(0, half, per_group):
            named = jnp.zeros((1, GROUP), F32)
            for s in range(first, first + per_group):

                @pl.when(all_remote | (mine != s))
                def _():
                    await_rows(kind, s)

                named = named + ids_in[kind, s]
            total = total + dot(
                hot(slot_iota == named),
                arrived[kind, first : first + per_group].reshape(GROUP, width),
            )
        return total

    def relay(i, receiver):
        return pltpu.make_async_remote_copy(
            src_ref=relay_out.at[i],
            dst_ref=relay_in,
            send_sem=relay_send.at[i],
            recv_sem=relay_recv.at[0],
            device_id={"mesh": receiver},
            device_id_type=MESH,
        )

    relays = (relay(0, far_inner * quarter + place_in), relay(1, far_outer * quarter + place_in))
    direct = jnp.where(core == DIRECT, 1, 0)

    @pl.when(inner == 1)
    def _():
        relay_out[0] = collect(0, False).astype(BF16)
        relays[0].start()

    @pl.when(inner * (1 - direct) == 1)
    def _():
        relay_out[1] = collect(1, False).astype(BF16)
        relays[1].start()

    @pl.when((1 - inner) * direct == 1)
    def _():
        relay_in[...] = collect(1, True).astype(BF16)

    gathered = collect(2, False)

    @pl.when((1 - inner) * direct == 0)
    def _():
        relays[0].wait_recv()

    gathered = gathered + relay_in[...].astype(F32)

    state = update(embed[...], prepared, gathered, w_enc_first, w_enc_second)
    sent = dot(state, w_send[...]).astype(BF16)
    inner_rows = half * hcap

    def list_rows(side):
        rows = dot(list_hot[pl.ds(side * inner_rows, inner_rows), :], sent)
        halo_out[pl.ds(side * half, half)] = rows.astype(BF16).reshape(half, hcap, width)

    list_rows(1 - h)

    def halo_copy(b, slot, receiver):
        return pltpu.make_async_remote_copy(
            src_ref=halo_out.at[receiver],
            dst_ref=halo_in.at[slot],
            send_sem=halo_send.at[b],
            recv_sem=halo_recv.at[slot],
            device_id={"mesh": receiver},
            device_id_type=MESH,
        )

    sent_halos = []
    for b in range(n):
        if b == half:
            list_rows(h)
        kind, side = HALO_ORDER[b // chips]
        receiver = by_class[kind] * quarter + column(b, side, 1)
        copy = halo_copy(b, mine + half if kind < 2 else mine, receiver)
        if kind == 3 and (b + 1) % chips == 0:
            own = core == side
            sent_halos.append((copy, own))

            @pl.when(jnp.logical_not(own))
            def _():
                copy.start()
        else:
            sent_halos.append((copy, None))
            copy.start()
    halo_in[mine] = halo_out[me]
    local_table[:nodes, :] = sent
    local_table[nodes:, :] = dot(state, w_recv[...]).astype(BF16)
    for chunk in range(edge_count // CHUNK):
        rows = pl.ds(chunk * CHUNK, CHUNK)
        pre[rows, :] += dot(near_hot[rows, :], local_table[...])

    for i in (15, 16, 17):
        loads[i].wait()
    prepared = prepare(state, w_proc_first)
    for s in range(half):

        @pl.when(mine != s)
        def _():
            halo_copy(0, s, other).wait_recv()

    halo = halo_in[:half].reshape(inner_rows, width)
    for chunk in range(edge_count // CHUNK):
        rows = pl.ds(chunk * CHUNK, CHUNK)
        pre[rows, :] += dot(halo_hot[rows, :inner_rows], halo)
    for s in range(half, n):
        halo_copy(0, s, other).wait_recv()
    halo = halo_in[half:].reshape(inner_rows, width)
    summed = jnp.zeros((nodes, width), F32)
    for chunk in range(edge_count // CHUNK):
        rows = pl.ds(chunk * CHUNK, CHUNK)
        edge_pre = pre[rows, :] + dot(halo_hot[rows, inner_rows:], halo)
        summed = summed + dot(
            node_hot[:, chunk * CHUNK : (chunk + 1) * CHUNK], silu(edge_pre).astype(BF16)
        )
    node_sum = dot(summed.astype(BF16), w_message[...])
    out_ref[...] = update(state, prepared, node_sum, w_proc_first, w_proc_second)

    @pl.when(inner == 1)
    def _():
        relays[0].wait_send()

    @pl.when(inner * (1 - direct) == 1)
    def _():
        relays[1].wait_send()

    for copies, own in sent_rows:
        if own is None:
            copies[0].wait_send()
            copies[1].wait_send()
        else:

            @pl.when(jnp.logical_not(own))
            def _():
                copies[0].wait_send()
                copies[1].wait_send()

    for copy, own in sent_halos:
        if own is None:
            copy.wait_send()
        else:

            @pl.when(jnp.logical_not(own))
            def _():
                copy.wait_send()


def per_device(
    grid_in, owner, node_slot, mesh_embed, edge_latent, senders, receivers, send_list, *weights
):
    n = lax.axis_size("mesh")
    grid_count = grid_in.shape[0]
    nodes, width = mesh_embed.shape
    edge_count = edge_latent.shape[0]
    list_size = send_list.shape[1]
    cap = max(16, 2 * grid_count // n)
    hcap = max(16, list_size)
    if hcap != list_size:
        beyond = jnp.maximum(senders - nodes, 0)
        moved = nodes + beyond // list_size * hcap + beyond % list_size
        senders = jnp.where(senders < nodes, senders, moved)
        send_list = jnp.pad(send_list, ((0, 0), (0, hcap - list_size)))
    inputs = (
        grid_in.T,
        owner.reshape(1, grid_count),
        node_slot.reshape(1, grid_count),
        mesh_embed,
        edge_latent,
        senders.reshape(edge_count // LANES, LANES),
        receivers.reshape(edge_count // LANES, LANES),
        send_list,
    ) + weights
    dma = pltpu.SemaphoreType.DMA
    scratch = [pltpu.VMEM(x.shape, x.dtype) for x in inputs] + [
        pltpu.VMEM((grid_count, width), BF16),
        pltpu.VMEM((n, cap, width), BF16),
        pltpu.VMEM((3, n // 2, cap, width), BF16),
        pltpu.VMEM((n, 1, GROUP), F32),
        pltpu.VMEM((3, n // 2, 1, GROUP), F32),
        pltpu.VMEM((edge_count, width), F32),
        pltpu.VMEM((2 * nodes, width), BF16),
        pltpu.VMEM((edge_count, 2 * nodes), BF16),
        pltpu.VMEM((edge_count, n * hcap), BF16),
        pltpu.VMEM((nodes, edge_count), BF16),
        pltpu.VMEM((n * hcap, nodes), BF16),
        pltpu.VMEM((n, hcap, width), BF16),
        pltpu.VMEM((n, hcap, width), BF16),
        pltpu.VMEM((2, nodes, width), BF16),
        pltpu.VMEM((nodes, width), BF16),
        dma((2,)),
        dma((1,)),
        dma((len(inputs),)),
        dma((n,)),
        dma((3, n // 2)),
        dma((n,)),
        dma((3, n // 2)),
        dma((n,)),
        dma((n,)),
    ]
    return pl.pallas_call(
        functools.partial(kernel, n, cap, hcap),
        out_shape=jax.ShapeDtypeStruct((nodes, width), BF16),
        in_specs=[pl.BlockSpec(memory_space=pl.ANY)] * len(inputs),
        out_specs=pl.BlockSpec(memory_space=pltpu.VMEM),
        scratch_shapes=scratch,
        compiler_params=pltpu.CompilerParams(
            collective_id=0, has_side_effects=True, vmem_limit_bytes=56 << 20
        ),
    )(*inputs)


def solution(mesh):
    rows, split, full = P(("groups", "mesh"), None), P("mesh"), P()
    in_specs = (rows, split, split, rows, rows, split, split, split) + (full,) * 10
    return jax.shard_map(
        per_device, mesh=mesh, in_specs=in_specs, out_specs=rows, check_vma=False
    )
```

```python
import functools

import jax
import jax.numpy as jnp
from jax import lax
from jax.experimental import pallas as pl
from jax.experimental.pallas import tpu as pltpu
from jax.sharding import PartitionSpec as P

F32 = jnp.float32
BF16 = jnp.bfloat16
MESH = pl.DeviceIdType.MESH
GROUP = 256
CHUNK = 1024
LANES = 128
DIRECT = 0
ROW_ORDER = ((0, 1), (0, 0), (1, 0), (1, 1), (2, 1), (2, 0), (3, 1), (3, 0))
HALO_ORDER = (1, 0, 2, 3)


def dot(left, right):
    return jnp.dot(left, right, preferred_element_type=F32)


def silu(x):
    half = 0.5 * x
    return half * jnp.tanh(half) + half


def normalize(values):
    center = values - jnp.mean(values, -1, keepdims=True)
    spread = jnp.mean(center * center, -1, keepdims=True)
    return center * lax.rsqrt(spread + 1e-05)


def hot(flags):
    return jnp.where(flags, 1.0, 0.0).astype(BF16)


def prepare(state, w_first):
    width = state.shape[1]
    rows = state.astype(F32)
    mean = jnp.mean(rows, -1, keepdims=True)
    square = jnp.sum((rows - mean) * (rows - mean), -1, keepdims=True)
    top = w_first[:width, :]
    return mean, square, dot(state, top), dot(jnp.ones((8, width), BF16), top)[:1]


def update(state, prepared, gathered, w_first, w_second):
    width = state.shape[1]
    own_mean, square, product, columns = prepared
    mean = 0.5 * (own_mean + jnp.mean(gathered, -1, keepdims=True))
    low, high = own_mean - mean, gathered - mean
    spread = (
        square + width * (low * low) + jnp.sum(high * high, -1, keepdims=True)
    ) / (2 * width)
    scale = lax.rsqrt(spread + 1e-05)
    hidden = dot((high * scale).astype(BF16), w_first[width:, :])
    hidden = hidden + scale * (product - mean * columns)
    return (state.astype(F32) + dot(silu(hidden).astype(BF16), w_second[...])).astype(BF16)


def kernel(n, cap, hcap, *refs):
    hbm = refs[:18]
    out_ref = refs[18]
    (
        grid_in,
        owner,
        node_slot,
        embed,
        edges,
        senders,
        receivers,
        send_list,
        w_grid_first,
        w_grid_second,
        w_enc_first,
        w_enc_second,
        w_send,
        w_recv,
        w_edge,
        w_message,
        w_proc_first,
        w_proc_second,
    ) = vmem = refs[19:37]
    (
        latent,
        outgoing,
        arrived,
        ids_out,
        ids_in,
        pre,
        local_table,
        near_hot,
        halo_hot,
        node_hot,
        list_hot,
        halo_out,
        halo_in,
        relay_out,
        relay_in,
        relay_send,
        relay_recv,
        load_sem,
        row_send,
        row_recv,
        id_send,
        id_recv,
        halo_send,
        halo_recv,
    ) = refs[37:]
    grid_count = grid_in.shape[1]
    nodes, width = embed.shape
    edge_count = edges.shape[0]
    me = lax.axis_index("mesh")

    half, quarter, chips = n // 2, n // 4, n // 8
    q, place_in = me // quarter, me % quarter
    h = q // 2
    mine = me % half
    core = place_in % 2
    inner = (q + 1) // 2 % 2
    far_inner, far_outer, near_other = 2 - h, 3 - 3 * h, 4 * h + 1 - q
    near_inner = 1 + h
    other = lax.rem(me + half, n)
    by_class = (far_inner, far_outer, near_other, q)

    def column(j, side, first=0):
        return lax.rem(place_in // 2 + (j + first) % chips, chips) * 2 + side

    loads = [
        pltpu.make_async_copy(source, target, load_sem.at[i])
        for i, (source, target) in enumerate(zip(hbm, vmem))
    ]
    for i in (0, 8, 1, 2, 9, 14, 4, 3, 10, 11, 7, 12, 13, 5, 6, 15, 16, 17):
        loads[i].start()
    barrier = pltpu.get_barrier_semaphore()
    for t in range(1, n):
        pl.semaphore_signal(
            barrier, inc=1, device_id={"mesh": lax.rem(me + t, n)}, device_id_type=MESH
        )

    for i in (1, 2, 0, 8, 9):
        loads[i].wait()
    block = lax.broadcasted_iota(jnp.int32, (n, 1), 0)
    turn = block // chips
    target = column(block, 0, 1)
    for i, (kind, side) in enumerate(ROW_ORDER):
        target = target + jnp.where(turn == i, by_class[kind] * quarter + side, 0)
    flags = jnp.where(target == owner[...], 1.0, 0.0)
    earlier = hot(
        lax.broadcasted_iota(jnp.int32, (grid_count, grid_count), 0)
        < lax.broadcasted_iota(jnp.int32, (grid_count, grid_count), 1)
    )
    rank = dot(flags.astype(BF16), earlier) + (block * cap).astype(F32)
    place = jnp.sum(flags * rank, 0, keepdims=True).astype(jnp.int32)
    slots = (flags * (node_slot[...] + 1).astype(F32)).astype(BF16)
    per_group = GROUP // cap
    lane_hot = hot(
        lax.broadcasted_iota(jnp.int32, (GROUP, grid_count), 0)
        == place % cap + mine % per_group * cap
    )
    ids = lax.dot_general(slots, lane_hot, (((1,), (1,)), ((), ())), preferred_element_type=F32)
    for t in range(n):
        ids_out[t] = ids[t : t + 1, :]

    hidden = lax.dot_general(
        grid_in[...], w_grid_first[...], (((0,), (0,)), ((), ())), preferred_element_type=F32
    )
    hidden = silu(hidden).astype(BF16)
    latent[...] = normalize(dot(hidden, w_grid_second[...])).astype(BF16)

    pl.semaphore_wait(barrier, n - 1)

    def row_copies(b, kind, slot, receiver):
        return (
            pltpu.make_async_remote_copy(
                src_ref=ids_out.at[b],
                dst_ref=ids_in.at[kind, slot],
                send_sem=id_send.at[b],
                recv_sem=id_recv.at[kind, slot],
                device_id={"mesh": receiver},
                device_id_type=MESH,
            ),
            pltpu.make_async_remote_copy(
                src_ref=outgoing.at[b],
                dst_ref=arrived.at[kind, slot],
                send_sem=row_send.at[b],
                recv_sem=row_recv.at[kind, slot],
                device_id={"mesh": receiver},
                device_id_type=MESH,
            ),
        )

    sent_rows = []
    for b in range(n):
        if b % per_group == 0:
            pack = hot(
                lax.broadcasted_iota(jnp.int32, (GROUP, grid_count), 0) + b * cap == place
            )
            packed = dot(pack, latent[...]).astype(BF16)
            outgoing[b : b + per_group] = packed.reshape(per_group, cap, width)
        kind, side = ROW_ORDER[b // chips]
        col = column(b, side, 1)
        if kind == 0:
            receiver = near_inner * quarter + col
        elif kind == 1:
            receiver = (far_outer if side == DIRECT else near_inner) * quarter + col
        else:
            receiver = by_class[kind] * quarter + col
        slot_kind = min(kind, 2)
        copies = row_copies(b, slot_kind, mine, receiver)
        if (b + 1) % chips == 0 and kind != 2 and (kind, side) != (1, DIRECT):
            own = (core == side) & (True if kind == 3 else inner == 1)
            sent_rows.append((copies, own))

            @pl.when(own)
            def _():
                ids_in[slot_kind, mine] = ids_out[b]
                arrived[slot_kind, mine] = outgoing[b]

            @pl.when(jnp.logical_not(own))
            def _():
                copies[0].start()
                copies[1].start()
        else:
            sent_rows.append((copies, None))
            copies[0].start()
            copies[1].start()

    loads[14].wait()
    loads[4].wait()
    for chunk in range(edge_count // CHUNK):
        rows = pl.ds(chunk * CHUNK, CHUNK)
        pre[rows, :] = dot(edges[rows, :], w_edge[...])

    loads[5].wait()
    loads[6].wait()
    loads[7].wait()
    sender_columns = jnp.transpose(senders[...])
    receiver_columns = jnp.transpose(receivers[...])
    list_columns = jnp.transpose(send_list[...])
    near_iota = lax.broadcasted_iota(jnp.int32, (LANES, nodes), 1)
    lane = lax.broadcasted_iota(jnp.int32, (1, n * hcap), 1)
    halo_place = nodes + lax.rem(lane + h * (half * hcap), n * hcap)
    node_iota = lax.broadcasted_iota(jnp.int32, (nodes, LANES), 0)
    for part in range(edge_count // LANES):
        rows = pl.ds(part * LANES, LANES)
        sender = sender_columns[:, part : part + 1]
        receiver = receiver_columns[:, part : part + 1]
        near_hot[rows, :nodes] = hot(sender == near_iota)
        near_hot[rows, nodes:] = hot(receiver == near_iota)
        halo_hot[rows, :] = hot(sender == halo_place)
        node_hot[:, part * LANES : (part + 1) * LANES] = hot(
            receivers[part : part + 1, :] == node_iota
        )
    list_iota = lax.broadcasted_iota(jnp.int32, (hcap, nodes), 1)
    for p in range(n):
        list_hot[p * hcap : (p + 1) * hcap, :] = hot(list_columns[:, p : p + 1] == list_iota)

    for i in (3, 10, 11, 12, 13):
        loads[i].wait()
    prepared = prepare(embed[...], w_enc_first)
    slot_iota = lax.broadcasted_iota(jnp.int32, (nodes, GROUP), 0).astype(F32) + 1.0

    def await_rows(kind, slot):
        copies = row_copies(0, kind, slot, other)
        copies[0].wait_recv()
        copies[1].wait_recv()

    def collect(kind, all_remote):
        total = jnp.zeros((nodes, width), F32)
        for first in range(0, half, per_group):
            named = jnp.zeros((1, GROUP), F32)
            for s in range(first, first + per_group):

                @pl.when(all_remote | (mine != s))
                def _():
                    await_rows(kind, s)

                named = named + ids_in[kind, s]
            total = total + dot(
                hot(slot_iota == named),
                arrived[kind, first : first + per_group].reshape(GROUP, width),
            )
        return total

    def relay(i, receiver):
        return pltpu.make_async_remote_copy(
            src_ref=relay_out.at[i],
            dst_ref=relay_in,
            send_sem=relay_send.at[i],
            recv_sem=relay_recv.at[0],
            device_id={"mesh": receiver},
            device_id_type=MESH,
        )

    relays = (relay(0, far_inner * quarter + place_in), relay(1, far_outer * quarter + place_in))
    direct = jnp.where(core == DIRECT, 1, 0)

    @pl.when(inner == 1)
    def _():
        relay_out[0] = collect(0, False).astype(BF16)
        relays[0].start()

    @pl.when(inner * (1 - direct) == 1)
    def _():
        relay_out[1] = collect(1, False).astype(BF16)
        relays[1].start()

    @pl.when((1 - inner) * direct == 1)
    def _():
        relay_in[...] = collect(1, True).astype(BF16)

    gathered = collect(2, False)

    @pl.when((1 - inner) * direct == 0)
    def _():
        relays[0].wait_recv()

    gathered = gathered + relay_in[...].astype(F32)

    state = update(embed[...], prepared, gathered, w_enc_first, w_enc_second)
    sent = dot(state, w_send[...]).astype(BF16)
    inner_rows = half * hcap

    def list_rows(side):
        rows = dot(list_hot[pl.ds(side * inner_rows, inner_rows), :], sent)
        halo_out[pl.ds(side * half, half)] = rows.astype(BF16).reshape(half, hcap, width)

    list_rows(1 - h)

    def halo_copy(b, slot, receiver):
        return pltpu.make_async_remote_copy(
            src_ref=halo_out.at[receiver],
            dst_ref=halo_in.at[slot],
            send_sem=halo_send.at[b],
            recv_sem=halo_recv.at[slot],
            device_id={"mesh": receiver},
            device_id_type=MESH,
        )

    sent_halos = []
    for b in range(n):
        if b == half:
            list_rows(h)
        kind, side = HALO_ORDER[b // quarter], b % 2
        receiver = by_class[kind] * quarter + column(b // 2, side, 1)
        copy = halo_copy(b, mine + half if kind < 2 else mine, receiver)
        if kind == 3 and (b // 2 + 1) % chips == 0:
            own = core == side
            sent_halos.append((copy, own))

            @pl.when(jnp.logical_not(own))
            def _():
                copy.start()
        else:
            sent_halos.append((copy, None))
            copy.start()
    halo_in[mine] = halo_out[me]
    local_table[:nodes, :] = sent
    local_table[nodes:, :] = dot(state, w_recv[...]).astype(BF16)
    for chunk in range(edge_count // CHUNK):
        rows = pl.ds(chunk * CHUNK, CHUNK)
        pre[rows, :] += dot(near_hot[rows, :], local_table[...])

    for i in (15, 16, 17):
        loads[i].wait()
    prepared = prepare(state, w_proc_first)
    for s in range(half):

        @pl.when(mine != s)
        def _():
            halo_copy(0, s, other).wait_recv()

    halo = halo_in[:half].reshape(inner_rows, width)
    for chunk in range(edge_count // CHUNK):
        rows = pl.ds(chunk * CHUNK, CHUNK)
        pre[rows, :] += dot(halo_hot[rows, :inner_rows], halo)
    for s in range(half, n):
        halo_copy(0, s, other).wait_recv()
    halo = halo_in[half:].reshape(inner_rows, width)
    summed = jnp.zeros((nodes, width), F32)
    for chunk in range(edge_count // CHUNK):
        rows = pl.ds(chunk * CHUNK, CHUNK)
        edge_pre = pre[rows, :] + dot(halo_hot[rows, inner_rows:], halo)
        summed = summed + dot(
            node_hot[:, chunk * CHUNK : (chunk + 1) * CHUNK], silu(edge_pre).astype(BF16)
        )
    node_sum = dot(summed.astype(BF16), w_message[...])
    out_ref[...] = update(state, prepared, node_sum, w_proc_first, w_proc_second)

    @pl.when(inner == 1)
    def _():
        relays[0].wait_send()

    @pl.when(inner * (1 - direct) == 1)
    def _():
        relays[1].wait_send()

    for copies, own in sent_rows:
        if own is None:
            copies[0].wait_send()
            copies[1].wait_send()
        else:

            @pl.when(jnp.logical_not(own))
            def _():
                copies[0].wait_send()
                copies[1].wait_send()

    for copy, own in sent_halos:
        if own is None:
            copy.wait_send()
        else:

            @pl.when(jnp.logical_not(own))
            def _():
                copy.wait_send()


def per_device(
    grid_in, owner, node_slot, mesh_embed, edge_latent, senders, receivers, send_list, *weights
):
    n = lax.axis_size("mesh")
    grid_count = grid_in.shape[0]
    nodes, width = mesh_embed.shape
    edge_count = edge_latent.shape[0]
    list_size = send_list.shape[1]
    cap = max(16, 2 * grid_count // n)
    hcap = max(16, list_size)
    if hcap != list_size:
        beyond = jnp.maximum(senders - nodes, 0)
        moved = nodes + beyond // list_size * hcap + beyond % list_size
        senders = jnp.where(senders < nodes, senders, moved)
        send_list = jnp.pad(send_list, ((0, 0), (0, hcap - list_size)))
    inputs = (
        grid_in.T,
        owner.reshape(1, grid_count),
        node_slot.reshape(1, grid_count),
        mesh_embed,
        edge_latent,
        senders.reshape(edge_count // LANES, LANES),
        receivers.reshape(edge_count // LANES, LANES),
        send_list,
    ) + weights
    dma = pltpu.SemaphoreType.DMA
    scratch = [pltpu.VMEM(x.shape, x.dtype) for x in inputs] + [
        pltpu.VMEM((grid_count, width), BF16),
        pltpu.VMEM((n, cap, width), BF16),
        pltpu.VMEM((3, n // 2, cap, width), BF16),
        pltpu.VMEM((n, 1, GROUP), F32),
        pltpu.VMEM((3, n // 2, 1, GROUP), F32),
        pltpu.VMEM((edge_count, width), F32),
        pltpu.VMEM((2 * nodes, width), BF16),
        pltpu.VMEM((edge_count, 2 * nodes), BF16),
        pltpu.VMEM((edge_count, n * hcap), BF16),
        pltpu.VMEM((nodes, edge_count), BF16),
        pltpu.VMEM((n * hcap, nodes), BF16),
        pltpu.VMEM((n, hcap, width), BF16),
        pltpu.VMEM((n, hcap, width), BF16),
        pltpu.VMEM((2, nodes, width), BF16),
        pltpu.VMEM((nodes, width), BF16),
        dma((2,)),
        dma((1,)),
        dma((len(inputs),)),
        dma((n,)),
        dma((3, n // 2)),
        dma((n,)),
        dma((3, n // 2)),
        dma((n,)),
        dma((n,)),
    ]
    return pl.pallas_call(
        functools.partial(kernel, n, cap, hcap),
        out_shape=jax.ShapeDtypeStruct((nodes, width), BF16),
        in_specs=[pl.BlockSpec(memory_space=pl.ANY)] * len(inputs),
        out_specs=pl.BlockSpec(memory_space=pltpu.VMEM),
        scratch_shapes=scratch,
        compiler_params=pltpu.CompilerParams(
            collective_id=0, has_side_effects=True, vmem_limit_bytes=56 << 20
        ),
    )(*inputs)


def solution(mesh):
    rows, split, full = P(("groups", "mesh"), None), P("mesh"), P()
    in_specs = (rows, split, split, rows, rows, split, split, split) + (full,) * 10
    return jax.shard_map(
        per_device, mesh=mesh, in_specs=in_specs, out_specs=rows, check_vma=False
    )
```
